128 devices in a mesh: ep: 16 (over y, x_lo, core), edp: 8 (over z, x_hi).
Axes of the slice: x: 4 (x_hi: 2, x_lo: 2; x = x_hi * 2 + x_lo), y: 4, z: 4, core: 2. Of those that a mesh axis runs over, the one named last changes fastest.
Arguments:
- routed_hidden: bfloat16 [1, 16, 8192, 704], P(None, 'ep', 'edp'), may hold values from -6 to 6
- routed_grads: bfloat16 [1, 16, 8192, 2048], P(None, 'ep', 'edp'), may hold values from -6 to 6
- expert_counts: int32 [1, 8, 32], P(None, 'edp', 'ep'), may hold values from 1 to 512, as said below
- expert_offsets: int32 [1, 8, 32], P(None, 'edp', 'ep'), may hold values from 0 to 512, as said below
- attn_values: bfloat16 [1, 262144, 1024], P(None, ('ep', 'edp')), may hold values from -24 to 24
- attn_grads: bfloat16 [1, 262144, 2048], P(None, ('ep', 'edp')), may hold values from -6 to 6
- expert_master: float32 [1, 32, 704, 2048], P(None, 'ep', None, 'edp'), may hold values from -0.21875 to 0.21875
- expert_moment: float32 [1, 32, 704, 2048], P(None, 'ep', None, 'edp'), may hold values from -4 to 4
- expert_second: float32 [1, 32, 704, 2048], P(None, 'ep', None, 'edp'), may hold values from 0.1 to 2
- dense_master: float32 [1, 1024, 2048], P(None, ('ep', 'edp')), may hold values from -0.1875 to 0.1875
- dense_moment: float32 [1, 1024, 2048], P(None, ('ep', 'edp')), may hold values from -4 to 4
- dense_second: float32 [1, 1024, 2048], P(None, ('ep', 'edp')), may hold values from 0.1 to 2
Outputs:
- new_expert_master: float32 [1, 32, 704, 2048], P(None, 'ep', None, 'edp')
- new_expert_moment: float32 [1, 32, 704, 2048], P(None, 'ep', None, 'edp')
- new_expert_second: float32 [1, 32, 704, 2048], P(None, 'ep', None, 'edp')
- new_dense_master: float32 [1, 1024, 2048], P(None, ('ep', 'edp'))
- new_dense_moment: float32 [1, 1024, 2048], P(None, ('ep', 'edp'))
- new_dense_second: float32 [1, 1024, 2048], P(None, ('ep', 'edp'))
The draws below stay inside these ranges and needn't reach their ends.
Inputs may be any that keep to these rules, and one draw needn't show every extreme that they name: `expert_counts`: in every layer, all 2 experts of some ep index in some buffer have count 512. `expert_offsets`: the segments of the 2 experts of one ep index in one buffer lie one after another in some order: the first placed starts at 0 and each next one starts at the previous start plus the previous count rounded up to a multiple of 128.
All inputs are finite; a program needn't handle non-finite values.
Results may differ from the reference program's by a relative error of at most 0.02.
Values may be sent and summed in bfloat16 or wider, within the bound.
A program may use at most 128 MiB of HBM per device.

```python
import math
import jax
import jax.numpy as jnp
from jax import lax

D = 2048
FFW = 704
HW = 1024
LAYERS = 1
EXP_DEV = 2
CAP = 512
ROWS_DEV = 1024
EXPERTS = 32
TOKENS = 262144
N_EP = 16
N_EDP = 8


def route_plan(key):
    base = jax.random.fold_in(key, 7)
    key_one, key_two, key_three, key_four = jax.random.split(base, 4)
    shape = (LAYERS, N_EDP, EXPERTS)
    first_draw = jax.random.randint(key_one, shape, 0, CAP, dtype=jnp.int32)
    second_draw = jax.random.randint(key_two, shape, 0, CAP, dtype=jnp.int32)
    counts_all = 1 + first_draw * second_draw // CAP
    group_total = N_EDP * (EXPERTS // EXP_DEV)
    chosen = jax.random.randint(key_three, (LAYERS,), 0, group_total, dtype=jnp.int32)
    grouped_counts = counts_all.reshape(LAYERS, group_total, EXP_DEV)
    hit_mask = jnp.arange(group_total, dtype=jnp.int32)[None, :, None] == chosen[:, None, None]
    grouped_counts = jnp.where(hit_mask, CAP, grouped_counts)
    counts_all = grouped_counts.reshape(shape)
    blocks_used = (counts_all + 127) // 128
    grouped = blocks_used.reshape(LAYERS, N_EDP, EXPERTS // EXP_DEV, EXP_DEV)
    scores = jax.random.randint(key_four, grouped.shape, 0, 1024, dtype=jnp.int32) * EXP_DEV + jnp.arange(EXP_DEV, dtype=jnp.int32)
    order = jnp.argsort(scores, axis=-1, stable=True).astype(jnp.int32)
    place = jnp.argsort(order, axis=-1, stable=True).astype(jnp.int32)
    placed_blocks = jnp.take_along_axis(grouped, order, axis=-1)
    placed_starts = (jnp.cumsum(placed_blocks, axis=-1) - placed_blocks) * 128
    starts = jnp.take_along_axis(placed_starts, place, axis=-1)
    return (counts_all.astype(jnp.int32), starts.reshape(shape).astype(jnp.int32))


def draw_expert_counts(key, part):
    return route_plan(key)[0]


def draw_expert_offsets(key, part):
    return route_plan(key)[1]


def with_spikes(result, own_key, source, target, blocks, factor):
    def block_of(axis_at):
        return (jnp.arange(result.shape[axis_at]) // (result.shape[axis_at] // blocks)).reshape((-1,) + (1,) * (result.ndim - 1 - axis_at))

    first = jax.random.permutation(own_key, blocks)[block_of(target)]
    other_side = (block_of(target) + blocks // 2) % blocks
    return jnp.where((block_of(source) == first) | (block_of(source) == other_side), factor * result, result)


def levels(own_key, dims, cuts, low, largest):
    loudness = 1.0
    for dim, shards_of in cuts:
        draws = jax.random.uniform(jax.random.fold_in(jax.random.fold_in(own_key, 6), dim), (shards_of,), jnp.float32, low / len(cuts), largest / len(cuts))
        loudness = loudness * jnp.repeat(jnp.exp(draws), dims[dim] // shards_of).reshape((-1,) + (1,) * (len(dims) - 1 - dim))
    return loudness


def gaussian(own_key, shape, width, limit, cuts=(), held_as=jnp.bfloat16):
    array = jax.random.normal(own_key, shape, jnp.float32) * width
    if len(cuts) > 0:
        array = levels(own_key, shape, cuts, -0.22, 0.18) * array
    return jnp.clip(array, min=-limit, max=limit).astype(held_as)


def bell_draw_with(own_key, extent, scale, limit, shards, heavy, held_as=jnp.bfloat16):
    values = scale * jax.random.normal(own_key, extent, jnp.float32)
    if shards:
        values = values * levels(own_key, extent, shards, -0.22, 0.18)
    return jnp.clip(with_spikes(values, jax.random.fold_in(own_key, 3), *heavy), -limit, limit).astype(held_as)


def setup_inputs(seed: int = 0) -> dict:
    streams_of = jax.random.split(jax.random.key(seed), 13)
    routed_hidden = gaussian(streams_of[0], (LAYERS, N_EP, N_EDP * ROWS_DEV, FFW), 1.0, 6.0, ((1, 16), (2, 8)))
    routed_grads = bell_draw_with(streams_of[1], (LAYERS, N_EP, N_EDP * ROWS_DEV, D), 1.0, 6.0, ((1, 16), (2, 8)), (2, 3, 8, 2.0))
    expert_counts = draw_expert_counts(jax.random.fold_in(streams_of[12], 71), 0)
    expert_offsets = draw_expert_offsets(jax.random.fold_in(streams_of[12], 71), 0)
    attn_values = bell_draw_with(streams_of[4], (LAYERS, TOKENS, HW), 1.0, 24.0, ((1, 128),), (1, 2, 128, 5.5))
    attn_grads = gaussian(streams_of[5], (LAYERS, TOKENS, D), 1.0, 6.0, ((1, 128),))
    expert_master = gaussian(streams_of[6], (LAYERS, EXPERTS, FFW, D), FFW ** -0.5, 0.21875, ((1, 16), (3, 8)), jnp.float32)
    expert_moment = gaussian(streams_of[7], (LAYERS, EXPERTS, FFW, D), 0.5, 4.0, ((1, 16), (3, 8)), jnp.float32)
    expert_second = jnp.clip(jnp.exp(math.log(2.0) - 2.9957323 * jax.random.uniform(streams_of[8], (LAYERS, EXPERTS, FFW, D), jnp.float32) ** levels(streams_of[8], (LAYERS, EXPERTS, FFW, D), ((1, 16), (3, 8)), -0.2, 0.2)), 0.1, 2.0)
    dense_master = gaussian(streams_of[9], (LAYERS, HW, D), HW ** -0.5, 0.1875, ((1, 128),), jnp.float32)
    dense_moment = gaussian(streams_of[10], (LAYERS, HW, D), 0.5, 4.0, ((1, 128),), jnp.float32)
    dense_second = jnp.clip(jnp.exp(math.log(2.0) - 2.9957323 * jax.random.uniform(streams_of[11], (LAYERS, HW, D), jnp.float32) ** levels(streams_of[11], (LAYERS, HW, D), ((1, 128),), -0.2, 0.2)), 0.1, 2.0)
    return dict(routed_hidden=routed_hidden, routed_grads=routed_grads, expert_counts=expert_counts, expert_offsets=expert_offsets, attn_values=attn_values, attn_grads=attn_grads, expert_master=expert_master, expert_moment=expert_moment, expert_second=expert_second, dense_master=dense_master, dense_moment=dense_moment, dense_second=dense_second)


beta_one = 0.9
beta_two = 0.95
adam_step = 10.0
adam_eps = 1e-08
learn_rate = 0.01
decay_rate = 0.1

def adamw(master, moment, second, grad, factor):
    clipped = grad * factor
    new_moment = beta_one * moment + (1.0 - beta_one) * clipped
    new_second = beta_two * second + (1.0 - beta_two) * clipped * clipped
    corr_one = 1.0 - beta_one ** adam_step
    corr_two = 1.0 - beta_two ** adam_step
    update = new_moment / corr_one / (jnp.sqrt(new_second / corr_two) + adam_eps) + decay_rate * master
    return (master - learn_rate * update, new_moment, new_second)

def reference(routed_hidden, routed_grads, expert_counts, expert_offsets, attn_values, attn_grads, expert_master, expert_moment, expert_second, dense_master, dense_moment, dense_second):

    def expert_grad(flat):
        layer_idx = flat // EXPERTS
        expert_idx = flat % EXPERTS
        group = expert_idx // EXP_DEV
        hidden_all = routed_hidden[layer_idx, group]
        grads_all = routed_grads[layer_idx, group]

        def add_part(part_idx, total):
            part_idx = part_idx.astype(jnp.int32)
            row_count = expert_counts[layer_idx, part_idx, expert_idx]
            row_start = expert_offsets[layer_idx, part_idx, expert_idx]
            hidden_blk = lax.dynamic_slice_in_dim(hidden_all, (part_idx * ROWS_DEV).astype(jnp.int32), ROWS_DEV, 0)
            grads_blk = lax.dynamic_slice_in_dim(grads_all, (part_idx * ROWS_DEV).astype(jnp.int32), ROWS_DEV, 0)
            hidden_blk = jnp.concatenate([hidden_blk, jnp.zeros((CAP, FFW), hidden_blk.dtype)], 0)
            grads_blk = jnp.concatenate([grads_blk, jnp.zeros((CAP, D), grads_blk.dtype)], 0)
            hidden_seg = lax.dynamic_slice_in_dim(hidden_blk, row_start.astype(jnp.int32), CAP, 0)
            grads_seg = lax.dynamic_slice_in_dim(grads_blk, row_start.astype(jnp.int32), CAP, 0)
            row_keep = (jnp.arange(CAP, dtype=jnp.int32) < row_count).astype(hidden_seg.dtype)
            term = lax.dot_general(hidden_seg * row_keep[:, None], grads_seg, (((0,), (0,)), ((), ())), preferred_element_type=jnp.float32)
            rounded = lax.optimization_barrier(term.astype(jnp.bfloat16))
            return total + rounded.astype(jnp.float32)
        return lax.fori_loop(0, N_EDP, add_part, jnp.zeros((FFW, D), jnp.float32))
    flat_ids = jnp.arange(LAYERS * EXPERTS, dtype=jnp.int32)
    expert_total = lax.map(expert_grad, flat_ids).reshape(LAYERS, EXPERTS, FFW, D)
    dense_total = jnp.stack([lax.dot_general(attn_values[idx], attn_grads[idx], (((0,), (0,)), ((), ())), preferred_element_type=jnp.float32) for idx in range(LAYERS)])
    squares = jnp.sum(expert_total * expert_total) + jnp.sum(dense_total * dense_total)
    total_count = float(LAYERS * EXPERTS * FFW * D + LAYERS * HW * D)
    factor = jnp.minimum(1.0, jnp.sqrt(total_count) / (jnp.sqrt(squares) + 1e-06))
    new_em, new_emo, new_es = adamw(expert_master, expert_moment, expert_second, expert_total, factor)
    new_dm, new_dmo, new_ds = adamw(dense_master, dense_moment, dense_second, dense_total, factor)
    return (new_em, new_emo, new_es, new_dm, new_dmo, new_ds)
```

```python
import jax
import jax.numpy as jnp
from jax import lax
from jax.experimental import pallas as pl
from jax.experimental.pallas import tpu as pltpu
from jax.sharding import PartitionSpec as P

D = 2048
FFW = 704
HW = 1024
LAYERS = 1
EXP_DEV = 2
HALF = FFW // 2
NCOL = 2
WCOL = D // NCOL

beta_one = 0.9
beta_two = 0.95
adam_step = 10.0
adam_eps = 1e-08
learn_rate = 0.01
decay_rate = 0.1

MESH = pl.DeviceIdType.MESH
TRANS = (((0,), (0,)), ((), ()))


def adamw(master, moment, second, grad, factor):
    clipped = grad * factor
    new_moment = beta_one * moment + (1.0 - beta_one) * clipped
    new_second = beta_two * second + (1.0 - beta_two) * clipped * clipped
    corr_one = 1.0 - beta_one**adam_step
    corr_two = 1.0 - beta_two**adam_step
    update = (
        new_moment / corr_one / (jnp.sqrt(new_second / corr_two) + adam_eps) + decay_rate * master
    )
    return (master - learn_rate * update, new_moment, new_second)


def grad_kernel(
    total_count,
    counts,
    offsets,
    hid_hbm,
    grd_hbm,
    val_hbm,
    att_hbm,
    exp_out,
    den_out,
    fac_out,
    hid,
    grd,
    val,
    att,
    hmask,
    part_a,
    part_b,
    recv_bx,
    fwd_a,
    cmb_a,
    dir_a,
    send_ax,
    recv_ax,
    fwd_b,
    cmb_b,
    dir_b,
    part_d,
    acc_d,
    fwd_y,
    cmb_y,
    dir_y,
    fwd_z,
    cmb_z,
    dir_z,
    recv_dx,
    sq_own,
    sq_row,
    recv_n1,
    recv_n2,
    load_sem,
    send_sem,
    recv_sem,
):
    ep = lax.axis_index("ep")
    edp = lax.axis_index("edp")
    y = ep // 4
    xl = (ep // 2) % 2
    core = ep % 2
    z = edp // 2
    xh = edp % 2
    x = xh * 2 + xl

    def dev(px, py, pz, pc):
        return (py * 4 + (px % 2) * 2 + pc, pz * 2 + px // 2)

    sibling = dev(x, y, z, 1 - core)
    z_next = dev(x, y, (z + 1) % 4, core)
    z_prev = dev(x, y, (z + 3) % 4, core)
    y_next = dev(x, (y + 1) % 4, z, core)
    y_prev = dev(x, (y + 3) % 4, z, core)

    loads = []
    for i, (src, dst) in enumerate(
        ((hid_hbm, hid), (grd_hbm, grd), (att_hbm, att), (val_hbm, val))
    ):
        loads.append(pltpu.make_async_copy(src, dst, load_sem.at[i]))
        loads[-1].start()

    barrier = pltpu.get_barrier_semaphore()
    ep_peers = [((ep + k) % 16, edp) for k in range(1, 16)]
    edp_peers = [(ep, (edp + k) % 8) for k in range(1, 8)]
    x_other = [dev((1 - xh) * 2 + 1 - xl, y, z, core)]
    greeted = ep_peers + edp_peers + x_other
    for peer in greeted:
        pl.semaphore_signal(barrier, inc=1, device_id=peer, device_id_type=MESH)

    loads[0].wait()
    lane = lax.broadcasted_iota(jnp.int32, (FFW, 1024), 1)
    for e in range(EXP_DEV):
        rel = lane - offsets[e]
        keep = jnp.logical_and(rel >= 0, rel < counts[e])
        hmask[e] = jnp.where(keep, hid[...], jnp.zeros_like(hid))
    loads[1].wait()

    started = []
    free = iter(range(200))

    def copy(src, dst, peer):
        i = next(free)
        return pltpu.make_async_remote_copy(
            src_ref=src,
            dst_ref=dst,
            send_sem=send_sem.at[i],
            recv_sem=recv_sem.at[i],
            device_id=peer,
            device_id_type=MESH,
        )

    def go(c):
        c.start()
        started.append(c)

    class Ring:
        def __init__(self, nxt, prv, block, fwd, cmb, direct, add):
            self.block, self.fwd, self.cmb, self.direct, self.add = block, fwd, cmb, direct, add
            self.fwd_copy = [copy(block(2, 0), fwd(0), nxt), copy(block(2, 1), fwd(1), prv)]
            self.dir_copy = [copy(block(1, 1), direct(0), nxt), copy(block(3, 0), direct(1), prv)]
            self.cmb_copy = [copy(fwd(0), cmb(0), nxt), copy(fwd(1), cmb(1), prv)]

        def send_far(self):
            for c in self.fwd_copy:
                go(c)

        def send_near(self, d):
            go(self.dir_copy[d])

        def relay(self):
            for d in (0, 1):
                self.fwd_copy[d].wait_recv()
                self.add(self.fwd(d), [self.fwd(d), self.block((1, 3)[d], d)])
                go(self.cmb_copy[d])

        def wait(self):
            for c in self.cmb_copy + self.dir_copy:
                c.wait_recv()

        def terms(self, h):
            return [self.block(0, h), self.cmb(h), self.direct(1 - h)]

    def add_bf16(dst, srcs):
        rows = 32

        def step(i, carry):
            r = pl.ds(pl.multiple_of(i * rows, rows), rows)
            total = srcs[0][r, :].astype(jnp.float32)
            for s in srcs[1:]:
                total += s[r, :].astype(jnp.float32)
            dst[r, :] = total.astype(dst.dtype)
            return carry

        lax.fori_loop(0, dst.shape[0] // rows, step, 0)

    def add_f32(dst, srcs):
        rows = 8

        def step(i, carry):
            r = pl.ds(pl.multiple_of(i * rows, rows), rows)
            total = srcs[0][r, :]
            for s in srcs[1:]:
                total += s[r, :]
            dst[r, :] = total
            return carry

        lax.fori_loop(0, dst.shape[0] // rows, step, 0)

    x_far = dev((x + 2) % 4, y, z, core)
    ring_a = Ring(
        z_next,
        z_prev,
        lambda k, h: part_a.at[(z + k) % 4, pl.ds(h * HALF, HALF)],
        lambda d: fwd_a.at[d],
        lambda d: cmb_a.at[d],
        lambda d: dir_a.at[d],
        add_bf16,
    )
    ring_b = Ring(
        z_next,
        z_prev,
        lambda k, h: part_b.at[xh, (z + k) % 4, pl.ds(h * HALF, HALF)],
        lambda d: fwd_b.at[d],
        lambda d: cmb_b.at[d],
        lambda d: dir_b.at[d],
        add_bf16,
    )
    ax_copy = copy(send_ax, recv_ax, x_far)
    bx_copy = {
        k: copy(part_b.at[1 - xh, (z + k) % 4], recv_bx.at[(z + k) % 4], x_far)
        for k in (2, 1, 3, 0)
    }

    def expert_part(k):
        c = (z + k) % 4
        cols = pl.ds(pl.multiple_of(c * 512, 512), 512)
        for e in (1, 0):
            prod = jnp.dot(
                hmask[e], grd[:, cols], preferred_element_type=jnp.float32
            ).astype(jnp.bfloat16)
            if e == 0:
                part_a[c] = prod
            else:
                part_b[0, c] = prod[:, :256]
                part_b[1, c] = prod[:, 256:]
                if k == 2:
                    pl.semaphore_wait(barrier, len(greeted))
                go(bx_copy[k])

    expert_part(2)
    ring_a.send_far()
    expert_part(1)
    expert_part(3)
    ring_a.send_near(0)
    ring_a.send_near(1)
    expert_part(0)

    def cols_of(n):
        return pl.ds(n * WCOL, WCOL)

    d0_copy = {}
    ring_y, ring_z, dx_copy = [], [], []
    for n in range(NCOL):
        for k in range(4):
            c = (y + k) % 4
            d0_copy[k, n] = copy(
                part_d.at[c, :, 1 - core, :, cols_of(n)], acc_d.at[c, :, :, cols_of(n)], sibling
            )
        ring_y.append(
            Ring(
                y_next,
                y_prev,
                lambda k, h, n=n: acc_d.at[(y + k) % 4, h, :, cols_of(n)],
                lambda d, n=n: fwd_y.at[n, d],
                lambda d, n=n: cmb_y.at[n, d],
                lambda d, n=n: dir_y.at[n, d],
                add_f32,
            )
        )
        ring_z.append(
            Ring(
                z_next,
                z_prev,
                lambda k, h, n=n: acc_d.at[
                    y, h, pl.ds(pl.multiple_of((z + k) % 4 * 16, 16), 16), cols_of(n)
                ],
                lambda d, n=n: fwd_z.at[n, d],
                lambda d, n=n: cmb_z.at[n, d],
                lambda d, n=n: dir_z.at[n, d],
                add_f32,
            )
        )

        def x_block(k, n=n):
            t = (x + k) % 4
            r = pl.multiple_of(z * 16 + t // 2 * 8, 8)
            return acc_d.at[y, t % 2, pl.ds(r, 8), cols_of(n)]

        dx_copy.append(
            [copy(x_block(k), recv_dx.at[n, k - 1], dev((x + k) % 4, y, z, core)) for k in (1, 2, 3)]
        )

    def dense_part(k):
        c = (y + k) % 4
        lhs = val[:, pl.ds(pl.multiple_of(c * 256, 256), 256)]
        for n in range(NCOL):
            prod = lax.dot_general(lhs, att[:, cols_of(n)], TRANS, preferred_element_type=jnp.float32)
            part_d[c, :, :, :, cols_of(n)] = prod.reshape(2, 2, 64, WCOL)
            go(d0_copy[k, n])

    def dense_core_sum(k):
        c = (y + k) % 4
        for n in range(NCOL):
            d0_copy[k, n].wait_recv()
            for h in (0, 1):
                mine = acc_d.at[c, h, :, cols_of(n)]
                add_f32(mine, [mine, part_d.at[c, h, core, :, cols_of(n)]])
            if k == 2:
                ring_y[n].send_far()
            elif k == 1:
                ring_y[n].send_near(0)
            elif k == 3:
                ring_y[n].send_near(1)

    def fold_b(k):
        bx_copy[k].wait_recv()
        c = (z + k) % 4
        mine = part_b.at[xh, c]
        add_bf16(mine, [mine, recv_bx.at[c]])

    loads[2].wait()
    loads[3].wait()
    dense_part(2)
    dense_part(1)
    dense_core_sum(2)
    dense_part(3)
    dense_core_sum(1)
    fold_b(2)
    ring_b.send_far()
    dense_part(0)
    dense_core_sum(3)
    dense_core_sum(0)
    ring_a.relay()
    fold_b(1)
    ring_b.send_near(0)
    fold_b(3)
    ring_b.send_near(1)
    ring_y[0].relay()
    ring_b.relay()
    ring_y[1].relay()

    ring_a.wait()
    own = pl.ds(pl.multiple_of(xh * 256, 256), 256)
    far = pl.ds(pl.multiple_of((1 - xh) * 256, 256), 256)
    for h in (0, 1):
        terms = ring_a.terms(h)

        def step_a(i, carry, h=h, terms=terms):
            r = pl.ds(pl.multiple_of(i * 32, 32), 32)
            o = pl.ds(pl.multiple_of(h * HALF + i * 32, 32), 32)
            send = sum(t[r, far].astype(jnp.float32) for t in terms)
            send_ax[o, :] = send.astype(jnp.bfloat16)
            exp_out[0, o, :] = sum(t[r, own].astype(jnp.float32) for t in terms)
            return carry

        lax.fori_loop(0, HALF // 32, step_a, 0)
    go(ax_copy)

    def dense_y_done(n):
        ring_y[n].wait()
        for h in (0, 1):
            terms = ring_y[n].terms(h)
            add_f32(terms[0], terms)
        ring_z[n].send_far()
        ring_z[n].send_near(0)
        ring_z[n].send_near(1)

    def dense_z_done(n):
        ring_z[n].wait()
        for h in (0, 1):
            terms = ring_z[n].terms(h)
            add_f32(terms[0], terms)
        for c in dx_copy[n]:
            go(c)

    dense_y_done(0)

    fold_b(0)
    ring_b.wait()
    squares = jnp.zeros((32, 256), jnp.float32)
    for h in (0, 1):
        terms = ring_b.terms(h)

        def step_b(i, sq, h=h, terms=terms):
            r = pl.ds(pl.multiple_of(i * 32, 32), 32)
            o = pl.ds(pl.multiple_of(h * HALF + i * 32, 32), 32)
            total = sum(t[r, :].astype(jnp.float32) for t in terms)
            exp_out[1, o, :] = total
            return sq + total * total

        squares = lax.fori_loop(0, HALF // 32, step_b, squares)

    ring_z[0].relay()
    dense_y_done(1)
    dense_z_done(0)

    ax_copy.wait_recv()

    def step_c(i, sq):
        r = pl.ds(pl.multiple_of(i * 32, 32), 32)
        total = exp_out[0, r, :] + recv_ax[r, :].astype(jnp.float32)
        exp_out[0, r, :] = total
        return sq + total * total

    squares = lax.fori_loop(0, FFW // 32, step_c, squares)
    tile = squares[:, :128] + squares[:, 128:]
    tile = tile[0:8] + tile[8:16] + tile[16:24] + tile[24:32]

    ring_z[1].relay()
    dense_z_done(1)
    for n in range(NCOL):
        for c in dx_copy[n]:
            c.wait_recv()
        r = pl.multiple_of(z * 16 + xh * 8, 8)
        total = acc_d[y, xl, pl.ds(r, 8), cols_of(n)]
        for k in range(3):
            total = total + recv_dx[n, k]
        den_out[:, cols_of(n)] = total
        sq = total * total
        for j in range(WCOL // 128):
            tile = tile + sq[:, j * 128 : (j + 1) * 128]

    sq_own[...] = tile
    n1 = [copy(sq_own, recv_n1.at[k], edp_peers[k]) for k in range(7)]
    for c in n1:
        go(c)
    for k, c in enumerate(n1):
        c.wait_recv()
        tile = tile + recv_n1[k]
    sq_row[...] = tile
    n2 = [copy(sq_row, recv_n2.at[k], ep_peers[k]) for k in range(15)]
    for c in n2:
        go(c)
    for k, c in enumerate(n2):
        c.wait_recv()
        tile = tile + recv_n2[k]
    norm = jnp.sqrt(jnp.sum(jnp.sum(tile, axis=0, keepdims=True), axis=1, keepdims=True))
    factor = jnp.minimum(1.0, jnp.sqrt(jnp.full((1, 1), total_count, jnp.float32)) / (norm + 1e-06))
    fac_out[...] = jnp.broadcast_to(factor, (8, 128))

    for c in started:
        c.wait_send()


def summed_grads(hid_t, grd, counts, offsets, val, att, total_count):
    vm = pltpu.VMEM
    bf = jnp.bfloat16
    f32 = jnp.float32
    hbm = pl.BlockSpec(memory_space=pl.ANY)
    smem = pl.BlockSpec(memory_space=pltpu.SMEM)
    vmem = pl.BlockSpec(memory_space=pltpu.VMEM)
    return pl.pallas_call(
        lambda *refs: grad_kernel(total_count, *refs),
        name="summed_grads",
        out_shape=(
            jax.ShapeDtypeStruct((2, FFW, 256), f32),
            jax.ShapeDtypeStruct((8, D), f32),
            jax.ShapeDtypeStruct((8, 128), f32),
        ),
        in_specs=[smem, smem, hbm, hbm, hbm, hbm],
        out_specs=(vmem, vmem, vmem),
        scratch_shapes=[
            vm((FFW, 1024), bf),
            vm((1024, D), bf),
            vm((2048, HW), bf),
            vm((2048, D), bf),
            vm((2, FFW, 1024), bf),
            vm((4, FFW, 512), bf),
            vm((2, 4, FFW, 256), bf),
            vm((4, FFW, 256), bf),
            vm((2, HALF, 512), bf),
            vm((2, HALF, 512), bf),
            vm((2, HALF, 512), bf),
            vm((FFW, 256), bf),
            vm((FFW, 256), bf),
            vm((2, HALF, 256), bf),
            vm((2, HALF, 256), bf),
            vm((2, HALF, 256), bf),
            vm((4, 2, 2, 64, D), f32),
            vm((4, 2, 64, D), f32),
            vm((NCOL, 2, 64, WCOL), f32),
            vm((NCOL, 2, 64, WCOL), f32),
            vm((NCOL, 2, 64, WCOL), f32),
            vm((NCOL, 2, 16, WCOL), f32),
            vm((NCOL, 2, 16, WCOL), f32),
            vm((NCOL, 2, 16, WCOL), f32),
            vm((NCOL, 3, 8, WCOL), f32),
            vm((8, 128), f32),
            vm((8, 128), f32),
            vm((7, 8, 128), f32),
            vm((15, 8, 128), f32),
            pltpu.SemaphoreType.DMA((4,)),
            pltpu.SemaphoreType.DMA((96,)),
            pltpu.SemaphoreType.DMA((96,)),
        ],
        compiler_params=pltpu.CompilerParams(
            collective_id=0, has_side_effects=True, vmem_limit_bytes=60 << 20
        ),
    )(counts, offsets, hid_t, grd, val, att)


def body(
    routed_hidden,
    routed_grads,
    expert_counts,
    expert_offsets,
    attn_values,
    attn_grads,
    expert_master,
    expert_moment,
    expert_second,
    dense_master,
    dense_moment,
    dense_second,
):
    total_count = float(LAYERS * EXP_DEV * lax.axis_size("ep") * FFW * D + LAYERS * HW * D)
    expert_total, dense_total, factor = summed_grads(
        routed_hidden[0, 0].T,
        routed_grads[0, 0],
        expert_counts[0, 0],
        expert_offsets[0, 0],
        attn_values[0],
        attn_grads[0],
        total_count,
    )
    factor = factor[0, 0]
    new_em, new_emo, new_es = adamw(
        expert_master, expert_moment, expert_second, expert_total[None], factor
    )
    new_dm, new_dmo, new_ds = adamw(
        dense_master, dense_moment, dense_second, dense_total[None], factor
    )
    return (new_em, new_emo, new_es, new_dm, new_dmo, new_ds)


def solution(mesh):
    return jax.shard_map(
        body,
        mesh=mesh,
        in_specs=(
            P(None, "ep", "edp", None),
            P(None, "ep", "edp", None),
            P(None, "edp", "ep"),
            P(None, "edp", "ep"),
            P(None, ("ep", "edp"), None),
            P(None, ("ep", "edp"), None),
            P(None, "ep", None, "edp"),
            P(None, "ep", None, "edp"),
            P(None, "ep", None, "edp"),
            P(None, ("ep", "edp"), None),
            P(None, ("ep", "edp"), None),
            P(None, ("ep", "edp"), None),
        ),
        out_specs=(
            P(None, "ep", None, "edp"),
            P(None, "ep", None, "edp"),
            P(None, "ep", None, "edp"),
            P(None, ("ep", "edp"), None),
            P(None, ("ep", "edp"), None),
            P(None, ("ep", "edp"), None),
        ),
        check_vma=False,
    )
```

```python
import jax
import jax.numpy as jnp
from jax import lax
from jax.experimental import pallas as pl
from jax.experimental.pallas import tpu as pltpu
from jax.sharding import PartitionSpec as P

D = 2048
FFW = 704
HW = 1024
LAYERS = 1
EXP_DEV = 2
HALF = FFW // 2
NCOL = 4
WCOL = D // NCOL

beta_one = 0.9
beta_two = 0.95
adam_step = 10.0
adam_eps = 1e-08
learn_rate = 0.01
decay_rate = 0.1

MESH = pl.DeviceIdType.MESH
TRANS = (((0,), (0,)), ((), ()))


def adamw(master, moment, second, grad, factor):
    clipped = grad * factor
    new_moment = beta_one * moment + (1.0 - beta_one) * clipped
    new_second = beta_two * second + (1.0 - beta_two) * clipped * clipped
    corr_one = 1.0 - beta_one**adam_step
    corr_two = 1.0 - beta_two**adam_step
    update = (
        new_moment / corr_one / (jnp.sqrt(new_second / corr_two) + adam_eps) + decay_rate * master
    )
    return (master - learn_rate * update, new_moment, new_second)


def grad_kernel(
    total_count,
    counts,
    offsets,
    hid_hbm,
    grd_hbm,
    val_hbm,
    att_hbm,
    exp_out,
    den_out,
    fac_out,
    hid,
    grd,
    val,
    att,
    hmask,
    part_a,
    part_b,
    recv_bx,
    fwd_a,
    cmb_a,
    dir_a,
    send_ax,
    recv_ax,
    fwd_b,
    cmb_b,
    dir_b,
    part_d,
    acc_d,
    fwd_y,
    cmb_y,
    dir_y,
    fwd_z,
    cmb_z,
    dir_z,
    recv_dx,
    sq_own,
    sq_row,
    recv_n1,
    recv_n2,
    load_sem,
    send_sem,
    recv_sem,
):
    ep = lax.axis_index("ep")
    edp = lax.axis_index("edp")
    y = ep // 4
    xl = (ep // 2) % 2
    core = ep % 2
    z = edp // 2
    xh = edp % 2
    x = xh * 2 + xl

    def dev(px, py, pz, pc):
        return (py * 4 + (px % 2) * 2 + pc, pz * 2 + px // 2)

    sibling = dev(x, y, z, 1 - core)
    z_next = dev(x, y, (z + 1) % 4, core)
    z_prev = dev(x, y, (z + 3) % 4, core)
    y_next = dev(x, (y + 1) % 4, z, core)
    y_prev = dev(x, (y + 3) % 4, z, core)

    barrier = pltpu.get_barrier_semaphore()
    ep_peers = [((ep + k) % 16, edp) for k in range(1, 16)]
    edp_peers = [(ep, (edp + k) % 8) for k in range(1, 8)]
    x_peers = [dev((x + k) % 4, y, z, core) for k in (1, 2, 3)]
    greeted = [sibling, y_next, y_prev, z_next, z_prev] + x_peers
    for peer in greeted:
        pl.semaphore_signal(barrier, inc=1, device_id=peer, device_id_type=MESH)

    loads = {}

    def load(key, src, dst):
        loads[key] = pltpu.make_async_copy(src, dst, load_sem.at[len(loads)])
        loads[key].start()

    def load_columns(key, src, dst, start, width):
        cols = pl.ds(pl.multiple_of(start, width), width)
        load(key, src.at[:, cols], dst.at[:, cols])

    load("hid", hid_hbm, hid)
    load_columns(("grd", 2), grd_hbm, grd, (z + 2) % 4 * 512, 512)
    load_columns(("val", 2), val_hbm, val, (y + 2) % 4 * 256, 256)
    load_columns(("att", 0), att_hbm, att, 0, WCOL)
    for k in (1, 3, 0):
        load_columns(("val", k), val_hbm, val, (y + k) % 4 * 256, 256)
        load_columns(("grd", k), grd_hbm, grd, (z + k) % 4 * 512, 512)
        if k != 0:
            load_columns(("att", (k + 1) // 2), att_hbm, att, (k + 1) // 2 * WCOL, WCOL)
    load_columns(("att", 3), att_hbm, att, 3 * WCOL, WCOL)
    used = set()

    def loaded(*keys):
        for key in keys:
            if key not in used:
                used.add(key)
                loads[key].wait()

    loaded("hid")
    lane = lax.broadcasted_iota(jnp.int32, (FFW, 1024), 1)
    for e in range(EXP_DEV):
        rel = lane - offsets[e]
        keep = jnp.logical_and(rel >= 0, rel < counts[e])
        hmask[e] = jnp.where(keep, hid[...], jnp.zeros_like(hid))

    started = []
    free = iter(range(200))

    def copy(src, dst, peer):
        i = next(free)
        return pltpu.make_async_remote_copy(
            src_ref=src,
            dst_ref=dst,
            send_sem=send_sem.at[i],
            recv_sem=recv_sem.at[i],
            device_id=peer,
            device_id_type=MESH,
        )

    held = []

    def go(c):
        if held is not None:
            held.append(c)
        else:
            c.start()
        started.append(c)

    def enter():
        nonlocal held
        pl.semaphore_wait(barrier, len(greeted))
        for c in held:
            c.start()
        held = None

    class Ring:
        def __init__(self, nxt, prv, block, fwd, cmb, direct, add):
            self.block, self.fwd, self.cmb, self.direct, self.add = block, fwd, cmb, direct, add
            self.fwd_copy = [copy(block(2, 0), fwd(0), nxt), copy(block(2, 1), fwd(1), prv)]
            self.dir_copy = [copy(block(1, 1), direct(0), nxt), copy(block(3, 0), direct(1), prv)]
            self.cmb_copy = [copy(fwd(0), cmb(0), nxt), copy(fwd(1), cmb(1), prv)]

        def send_far(self):
            for c in self.fwd_copy:
                go(c)

        def send_near(self, d):
            go(self.dir_copy[d])

        def relay(self):
            for d in (0, 1):
                self.fwd_copy[d].wait_recv()
                self.add(self.fwd(d), [self.fwd(d), self.block((1, 3)[d], d)])
                go(self.cmb_copy[d])

        def wait(self):
            for c in self.cmb_copy + self.dir_copy:
                c.wait_recv()

        def terms(self, h):
            return [self.block(0, h), self.cmb(h), self.direct(1 - h)]

    def add_bf16(dst, srcs):
        rows = 32

        def step(i, carry):
            r = pl.ds(pl.multiple_of(i * rows, rows), rows)
            total = srcs[0][r, :].astype(jnp.float32)
            for s in srcs[1:]:
                total += s[r, :].astype(jnp.float32)
            dst[r, :] = total.astype(dst.dtype)
            return carry

        lax.fori_loop(0, dst.shape[0] // rows, step, 0)

    def add_f32(dst, srcs):
        rows = 16

        def step(i, carry):
            r = pl.ds(pl.multiple_of(i * rows, rows), rows)
            total = srcs[0][r, :]
            for s in srcs[1:]:
                total += s[r, :]
            dst[r, :] = total
            return carry

        lax.fori_loop(0, dst.shape[0] // rows, step, 0)

    x_far = x_peers[1]
    ring_a = Ring(
        z_next,
        z_prev,
        lambda k, h: part_a.at[(z + k) % 4, pl.ds(h * HALF, HALF)],
        lambda d: fwd_a.at[d],
        lambda d: cmb_a.at[d],
        lambda d: dir_a.at[d],
        add_bf16,
    )
    ring_b = Ring(
        z_next,
        z_prev,
        lambda k, h: part_b.at[xh, (z + k) % 4, pl.ds(h * HALF, HALF)],
        lambda d: fwd_b.at[d],
        lambda d: cmb_b.at[d],
        lambda d: dir_b.at[d],
        add_bf16,
    )
    ax_copy = copy(send_ax, recv_ax, x_far)
    bx_copy = {
        k: copy(part_b.at[1 - xh, (z + k) % 4], recv_bx.at[(z + k) % 4], x_far)
        for k in (2, 1, 3, 0)
    }

    def expert_part(k):
        c = (z + k) % 4
        cols = pl.ds(pl.multiple_of(c * 512, 512), 512)
        loaded(("grd", k))
        for e in (1, 0):
            prod = jnp.dot(
                hmask[e], grd[:, cols], preferred_element_type=jnp.float32
            ).astype(jnp.bfloat16)
            if e == 0:
                part_a[c] = prod
            else:
                part_b[0, c] = prod[:, :256]
                part_b[1, c] = prod[:, 256:]
                go(bx_copy[k])

    def cols_of(n):
        return pl.ds(n * WCOL, WCOL)

    d0_copy = {}
    ring_y, ring_z, dx_copy = [], [], []
    for n in range(NCOL):
        for k in range(4):
            c = (y + k) % 4
            d0_copy[k, n] = copy(
                part_d.at[c, :, 1 - core, :, cols_of(n)], acc_d.at[c, :, :, cols_of(n)], sibling
            )
        ring_y.append(
            Ring(
                y_next,
                y_prev,
                lambda k, h, n=n: acc_d.at[(y + k) % 4, h, :, cols_of(n)],
                lambda d, n=n: fwd_y.at[n, d],
                lambda d, n=n: cmb_y.at[n, d],
                lambda d, n=n: dir_y.at[n, d],
                add_f32,
            )
        )
        ring_z.append(
            Ring(
                z_next,
                z_prev,
                lambda k, h, n=n: acc_d.at[
                    y, h, pl.ds(pl.multiple_of((z + k) % 4 * 16, 16), 16), cols_of(n)
                ],
                lambda d, n=n: fwd_z.at[n, d],
                lambda d, n=n: cmb_z.at[n, d],
                lambda d, n=n: dir_z.at[n, d],
                add_f32,
            )
        )

        def x_block(k, n=n):
            t = (x + k) % 4
            r = pl.multiple_of(z * 16 + t // 2 * 8, 8)
            return acc_d.at[y, t % 2, pl.ds(r, 8), cols_of(n)]

        dx_copy.append(
            [copy(x_block(k), recv_dx.at[n, k - 1], dev((x + k) % 4, y, z, core)) for k in (1, 2, 3)]
        )

    def dense_part(k, n):
        c = (y + k) % 4
        loaded(("val", k), ("att", n))
        lhs = val[:, pl.ds(pl.multiple_of(c * 256, 256), 256)]
        prod = lax.dot_general(lhs, att[:, cols_of(n)], TRANS, preferred_element_type=jnp.float32)
        part_d[c, :, :, :, cols_of(n)] = prod.reshape(2, 2, 64, WCOL)
        go(d0_copy[k, n])

    def dense_core_sum(k, n):
        c = (y + k) % 4
        d0_copy[k, n].wait_recv()
        for h in (0, 1):
            mine = acc_d.at[c, h, :, cols_of(n)]
            add_f32(mine, [mine, part_d.at[c, h, core, :, cols_of(n)]])
        if k == 2:
            ring_y[n].send_far()
        elif k == 1:
            ring_y[n].send_near(0)
        elif k == 3:
            ring_y[n].send_near(1)

    def fold_b(k):
        bx_copy[k].wait_recv()
        c = (z + k) % 4
        mine = part_b.at[xh, c]
        add_bf16(mine, [mine, recv_bx.at[c]])

    own = pl.ds(pl.multiple_of(xh * 256, 256), 256)
    far = pl.ds(pl.multiple_of((1 - xh) * 256, 256), 256)

    def expert_a_done():
        ring_a.wait()
        for h in (0, 1):
            terms = ring_a.terms(h)

            def step_a(i, carry, h=h, terms=terms):
                r = pl.ds(pl.multiple_of(i * 32, 32), 32)
                o = pl.ds(pl.multiple_of(h * HALF + i * 32, 32), 32)
                send = sum(t[r, far].astype(jnp.float32) for t in terms)
                send_ax[o, :] = send.astype(jnp.bfloat16)
                exp_out[0, o, :] = sum(t[r, own].astype(jnp.float32) for t in terms)
                return carry

            lax.fori_loop(0, HALF // 32, step_a, 0)
        go(ax_copy)

    def dense_y_done(n):
        ring_y[n].wait()
        for h in (0, 1):
            terms = ring_y[n].terms(h)
            add_f32(terms[0], terms)
        ring_z[n].send_far()
        ring_z[n].send_near(0)
        ring_z[n].send_near(1)

    def dense_z_done(n):
        ring_z[n].wait()
        for h in (0, 1):
            terms = ring_z[n].terms(h)
            add_f32(terms[0], terms)
        for c in dx_copy[n]:
            go(c)

    sums = {"wide": jnp.zeros((32, 256), jnp.float32), "tile": jnp.zeros((8, 128), jnp.float32)}

    def expert_b_done():
        ring_b.wait()
        for h in (0, 1):
            terms = ring_b.terms(h)

            def step_b(i, sq, h=h, terms=terms):
                r = pl.ds(pl.multiple_of(i * 32, 32), 32)
                o = pl.ds(pl.multiple_of(h * HALF + i * 32, 32), 32)
                total = sum(t[r, :].astype(jnp.float32) for t in terms)
                exp_out[1, o, :] = total
                return sq + total * total

            sums["wide"] = lax.fori_loop(0, HALF // 32, step_b, sums["wide"])

    def expert_a_last():
        ax_copy.wait_recv()

        def step_c(i, sq):
            r = pl.ds(pl.multiple_of(i * 32, 32), 32)
            total = exp_out[0, r, :] + recv_ax[r, :].astype(jnp.float32)
            exp_out[0, r, :] = total
            return sq + total * total

        sums["wide"] = lax.fori_loop(0, FFW // 32, step_c, sums["wide"])

    def dense_last(n):
        for c in dx_copy[n]:
            c.wait_recv()
        r = pl.multiple_of(z * 16 + xh * 8, 8)
        total = acc_d[y, xl, pl.ds(r, 8), cols_of(n)]
        for k in range(3):
            total = total + recv_dx[n, k]
        den_out[:, cols_of(n)] = total
        sq = total * total
        for j in range(WCOL // 128):
            sums["tile"] = sums["tile"] + sq[:, j * 128 : (j + 1) * 128]

    expert_part(2)
    ring_a.send_far()
    dense_part(2, 1)
    dense_part(2, 0)
    enter()
    dense_part(3, 0)
    expert_part(3)
    dense_core_sum(2, 1)
    dense_part(1, 1)
    dense_part(3, 1)
    dense_core_sum(2, 0)
    ring_a.send_near(1)
    dense_part(1, 0)
    dense_core_sum(3, 1)
    expert_part(1)
    dense_core_sum(1, 0)
    dense_part(2, 2)
    ring_a.send_near(0)
    dense_core_sum(1, 1)
    dense_part(2, 3)
    dense_part(1, 2)
    dense_core_sum(3, 0)
    dense_part(0, 0)
    ring_y[1].relay()
    fold_b(2)
    dense_part(3, 3)
    ring_a.relay()
    dense_part(0, 1)
    dense_part(3, 2)
    ring_y[0].relay()
    dense_part(1, 3)
    dense_core_sum(2, 2)
    dense_core_sum(0, 0)
    dense_core_sum(1, 2)
    ring_b.send_far()
    expert_part(0)
    dense_core_sum(3, 3)
    dense_core_sum(2, 3)
    dense_y_done(0)
    dense_core_sum(3, 2)
    dense_part(0, 3)
    dense_core_sum(1, 3)
    fold_b(1)
    ring_y[2].relay()
    dense_part(0, 2)
    dense_core_sum(0, 1)
    expert_a_done()
    dense_core_sum(0, 2)
    dense_y_done(1)
    dense_core_sum(0, 3)
    fold_b(3)
    ring_y[3].relay()
    ring_z[0].relay()
    ring_b.relay()
    dense_y_done(2)
    dense_y_done(3)
    ring_z[2].relay()
    ring_z[1].relay()
    ring_z[3].relay()
    ring_b.send_near(0)
    ring_b.send_near(1)
    dense_z_done(0)
    fold_b(0)
    dense_z_done(2)
    expert_a_last()
    dense_z_done(1)
    dense_z_done(3)
    dense_last(1)
    dense_last(0)
    dense_last(2)
    expert_b_done()
    dense_last(3)

    tile = sums["wide"][:, :128] + sums["wide"][:, 128:]
    tile = sums["tile"] + tile[0:8] + tile[8:16] + tile[16:24] + tile[24:32]
    tile = jnp.sum(tile, axis=0, keepdims=True)
    sq_own[...] = tile
    n1 = [copy(sq_own, recv_n1.at[k], edp_peers[k]) for k in range(7)]
    for c in n1:
        go(c)
    for k, c in enumerate(n1):
        c.wait_recv()
        tile = tile + recv_n1[k]
    sq_row[...] = tile
    n2 = [copy(sq_row, recv_n2.at[k], ep_peers[k]) for k in range(15)]
    for c in n2:
        go(c)
    for k, c in enumerate(n2):
        c.wait_recv()
        tile = tile + recv_n2[k]
    norm = jnp.sqrt(jnp.sum(tile, axis=1, keepdims=True))
    factor = jnp.minimum(1.0, jnp.sqrt(jnp.full((1, 1), total_count, jnp.float32)) / (norm + 1e-06))
    fac_out[...] = jnp.broadcast_to(factor, (8, 128))

    for c in started:
        c.wait_send()


def summed_grads(hid_t, grd, counts, offsets, val, att, total_count):
    vm = pltpu.VMEM
    bf = jnp.bfloat16
    f32 = jnp.float32
    hbm = pl.BlockSpec(memory_space=pltpu.HBM)
    smem = pl.BlockSpec(memory_space=pltpu.SMEM)
    vmem = pl.BlockSpec(memory_space=pltpu.VMEM)
    return pl.pallas_call(
        lambda *refs: grad_kernel(total_count, *refs),
        name="summed_grads",
        out_shape=(
            jax.ShapeDtypeStruct((2, FFW, 256), f32),
            jax.ShapeDtypeStruct((8, D), f32),
            jax.ShapeDtypeStruct((8, 128), f32),
        ),
        in_specs=[smem, smem, hbm, hbm, hbm, hbm],
        out_specs=(vmem, vmem, vmem),
        scratch_shapes=[
            vm((FFW, 1024), bf),
            vm((1024, D), bf),
            vm((2048, HW), bf),
            vm((2048, D), bf),
            vm((2, FFW, 1024), bf),
            vm((4, FFW, 512), bf),
            vm((2, 4, FFW, 256), bf),
            vm((4, FFW, 256), bf),
            vm((2, HALF, 512), bf),
            vm((2, HALF, 512), bf),
            vm((2, HALF, 512), bf),
            vm((FFW, 256), bf),
            vm((FFW, 256), bf),
            vm((2, HALF, 256), bf),
            vm((2, HALF, 256), bf),
            vm((2, HALF, 256), bf),
            vm((4, 2, 2, 64, D), f32),
            vm((4, 2, 64, D), f32),
            vm((NCOL, 2, 64, WCOL), f32),
            vm((NCOL, 2, 64, WCOL), f32),
            vm((NCOL, 2, 64, WCOL), f32),
            vm((NCOL, 2, 16, WCOL), f32),
            vm((NCOL, 2, 16, WCOL), f32),
            vm((NCOL, 2, 16, WCOL), f32),
            vm((NCOL, 3, 8, WCOL), f32),
            vm((1, 128), f32),
            vm((1, 128), f32),
            vm((7, 1, 128), f32),
            vm((15, 1, 128), f32),
            pltpu.SemaphoreType.DMA((13,)),
            pltpu.SemaphoreType.DMA((115,)),
            pltpu.SemaphoreType.DMA((115,)),
        ],
        compiler_params=pltpu.CompilerParams(
            collective_id=0, has_side_effects=True, vmem_limit_bytes=52 << 20
        ),
    )(counts, offsets, hid_t, grd, val, att)


STEPS = 11


def adam_kernel(fac, eg, ew, em, es, dg, dw, dm, ds, *rest):
    outs, (ow, om, os_, pw, pm, ps), sem = rest[:6], rest[6:12], rest[12]
    factor = fac[0:1, 0:1]
    copies = []

    def out(src, dst):
        copies.append(pltpu.make_async_copy(src, dst, sem.at[len(copies)]))
        copies[-1].start()

    pw[...], pm[...], ps[...] = adamw(dw[...], dm[...], ds[...], dg[...], factor)
    for src, dst in zip((pw, pm, ps), outs[3:]):
        out(src, dst)
    rows = EXP_DEV * FFW // STEPS
    for i in range(STEPS):
        r = pl.ds(i * rows, rows)
        ow[r], om[r], os_[r] = adamw(ew[r], em[r], es[r], eg[r], factor)
        for src, dst in zip((ow, om, os_), outs[:3]):
            out(src.at[r], dst.at[r])
    for c in copies:
        c.wait()


def updated(factor, expert, dense):
    rows = EXP_DEV * FFW
    vmem = pl.BlockSpec(memory_space=pltpu.VMEM)
    hbm = pl.BlockSpec(memory_space=pl.ANY)
    return pl.pallas_call(
        adam_kernel,
        name="clipped_adamw",
        out_shape=[jax.ShapeDtypeStruct((rows, 256), jnp.float32)] * 3
        + [jax.ShapeDtypeStruct((8, D), jnp.float32)] * 3,
        in_specs=[vmem] * 9,
        out_specs=[hbm] * 6,
        scratch_shapes=[pltpu.VMEM((rows, 256), jnp.float32)] * 3
        + [pltpu.VMEM((8, D), jnp.float32)] * 3
        + [pltpu.SemaphoreType.DMA((3 * STEPS + 3,))],
        compiler_params=pltpu.CompilerParams(vmem_limit_bytes=16 << 20),
    )(factor, *expert, *dense)


def body(
    routed_hidden,
    routed_grads,
    expert_counts,
    expert_offsets,
    attn_values,
    attn_grads,
    expert_master,
    expert_moment,
    expert_second,
    dense_master,
    dense_moment,
    dense_second,
):
    total_count = float(LAYERS * EXP_DEV * lax.axis_size("ep") * FFW * D + LAYERS * HW * D)
    expert_total, dense_total, factor = summed_grads(
        routed_hidden[0, 0].T,
        routed_grads[0, 0],
        expert_counts[0, 0],
        expert_offsets[0, 0],
        attn_values[0],
        attn_grads[0],
        total_count,
    )
    expert = [
        a.reshape(EXP_DEV * FFW, 256)
        for a in (expert_total, expert_master, expert_moment, expert_second)
    ]
    dense = [a.reshape(8, D) for a in (dense_total, dense_master, dense_moment, dense_second)]
    new = updated(factor, expert, dense)
    return tuple(a.reshape(expert_master.shape) for a in new[:3]) + tuple(
        a.reshape(dense_master.shape) for a in new[3:]
    )


def solution(mesh):
    return jax.shard_map(
        body,
        mesh=mesh,
        in_specs=(
            P(None, "ep", "edp", None),
            P(None, "ep", "edp", None),
            P(None, "edp", "ep"),
            P(None, "edp", "ep"),
            P(None, ("ep", "edp"), None),
            P(None, ("ep", "edp"), None),
            P(None, "ep", None, "edp"),
            P(None, "ep", None, "edp"),
            P(None, "ep", None, "edp"),
            P(None, ("ep", "edp"), None),
            P(None, ("ep", "edp"), None),
            P(None, ("ep", "edp"), None),
        ),
        out_specs=(
            P(None, "ep", None, "edp"),
            P(None, "ep", None, "edp"),
            P(None, "ep", None, "edp"),
            P(None, ("ep", "edp"), None),
            P(None, ("ep", "edp"), None),
            P(None, ("ep", "edp"), None),
        ),
        check_vma=False,
    )
```

```python
import jax
import jax.numpy as jnp
from jax import lax
from jax.experimental import pallas as pl
from jax.experimental.pallas import tpu as pltpu
from jax.sharding import PartitionSpec as P

D = 2048
FFW = 704
HW = 1024
LAYERS = 1
EXP_DEV = 2
HALF = FFW // 2
WIDTHS = (512, 768, 512, 256)
NCOL = len(WIDTHS)
DIRECT = (2, 3)

beta_one = 0.9
beta_two = 0.95
adam_step = 10.0
adam_eps = 1e-08
learn_rate = 0.01
decay_rate = 0.1

MESH = pl.DeviceIdType.MESH
TRANS = (((0,), (0,)), ((), ()))


def adamw(master, moment, second, grad, factor):
    clipped = grad * factor
    new_moment = beta_one * moment + (1.0 - beta_one) * clipped
    new_second = beta_two * second + (1.0 - beta_two) * clipped * clipped
    corr_one = 1.0 - beta_one**adam_step
    corr_two = 1.0 - beta_two**adam_step
    update = (
        new_moment / corr_one / (jnp.sqrt(new_second / corr_two) + adam_eps) + decay_rate * master
    )
    return (master - learn_rate * update, new_moment, new_second)


def grad_kernel(
    total_count,
    counts,
    offsets,
    hid_hbm,
    grd_hbm,
    val_hbm,
    att_hbm,
    exp_out,
    den_out,
    fac_out,
    hid,
    grd,
    val,
    att,
    hmask,
    part_a,
    part_b,
    recv_bx,
    fwd_a,
    cmb_a,
    dir_a,
    send_ax,
    recv_ax,
    fwd_b,
    cmb_b,
    dir_b,
    part_d,
    acc_d,
    fwd_y,
    cmb_y,
    dir_y,
    fwd_z,
    cmb_z,
    dir_z,
    recv_dx,
    sq_own,
    sq_row,
    recv_n1,
    recv_n2,
    load_sem,
    send_sem,
    recv_sem,
):
    ep = lax.axis_index("ep")
    edp = lax.axis_index("edp")
    y = ep // 4
    xl = (ep // 2) % 2
    core = ep % 2
    z = edp // 2
    xh = edp % 2
    x = xh * 2 + xl

    def dev(px, py, pz, pc):
        return (py * 4 + (px % 2) * 2 + pc, pz * 2 + px // 2)

    sibling = dev(x, y, z, 1 - core)
    z_next = dev(x, y, (z + 1) % 4, core)
    z_prev = dev(x, y, (z + 3) % 4, core)
    y_next = dev(x, (y + 1) % 4, z, core)
    y_prev = dev(x, (y + 3) % 4, z, core)

    barrier = pltpu.get_barrier_semaphore()
    ep_peers = [((ep + k) % 16, edp) for k in range(1, 16)]
    edp_peers = [(ep, (edp + k) % 8) for k in range(1, 8)]
    x_peers = [dev((x + k) % 4, y, z, core) for k in (1, 2, 3)]
    greeted = [sibling, y_next, y_prev, z_next, z_prev] + x_peers
    for peer in greeted:
        pl.semaphore_signal(barrier, inc=1, device_id=peer, device_id_type=MESH)

    def cols_of(n):
        return pl.ds(sum(WIDTHS[:n]), WIDTHS[n])

    loads = {}

    def load(key, src, dst):
        loads[key] = pltpu.make_async_copy(src, dst, load_sem.at[len(loads)])
        loads[key].start()

    def load_columns(key, src, dst, start, width):
        cols = pl.ds(pl.multiple_of(start, width), width)
        load(key, src.at[:, cols], dst.at[:, cols])

    load("hid", hid_hbm, hid)
    load_columns(("grd", 2), grd_hbm, grd, (z + 2) % 4 * 512, 512)
    load_columns(("val", 2), val_hbm, val, (y + 2) % 4 * 256, 256)
    load(("att", 0), att_hbm.at[:, cols_of(0)], att.at[:, cols_of(0)])
    for k in (1, 3, 0):
        load_columns(("val", k), val_hbm, val, (y + k) % 4 * 256, 256)
        load_columns(("grd", k), grd_hbm, grd, (z + k) % 4 * 512, 512)
        if k != 0:
            n = (k + 1) // 2
            load(("att", n), att_hbm.at[:, cols_of(n)], att.at[:, cols_of(n)])
    load(("att", 3), att_hbm.at[:, cols_of(3)], att.at[:, cols_of(3)])
    used = set()

    def loaded(*keys):
        for key in keys:
            if key not in used:
                used.add(key)
                loads[key].wait()

    loaded("hid")
    lane = lax.broadcasted_iota(jnp.int32, (FFW, 1024), 1)
    for e in range(EXP_DEV):
        rel = lane - offsets[e]
        keep = jnp.logical_and(rel >= 0, rel < counts[e])
        hmask[e] = jnp.where(keep, hid[...], jnp.zeros_like(hid))

    started = []
    free = iter(range(200))

    def copy(src, dst, peer):
        i = next(free)
        return pltpu.make_async_remote_copy(
            src_ref=src,
            dst_ref=dst,
            send_sem=send_sem.at[i],
            recv_sem=recv_sem.at[i],
            device_id=peer,
            device_id_type=MESH,
        )

    held = []

    def go(c):
        if held is not None:
            held.append(c)
        else:
            c.start()
        started.append(c)

    def enter():
        nonlocal held
        pl.semaphore_wait(barrier, len(greeted))
        for c in held:
            c.start()
        held = None

    def settle():
        while started:
            started.pop(0).wait_send()

    class Ring:
        def __init__(self, nxt, prv, block, fwd, cmb, direct, add):
            self.block, self.fwd, self.cmb, self.direct, self.add = block, fwd, cmb, direct, add
            self.fwd_copy = [copy(block(2, 0), fwd(0), nxt), copy(block(2, 1), fwd(1), prv)]
            self.dir_copy = [copy(block(1, 1), direct(0), nxt), copy(block(3, 0), direct(1), prv)]
            self.cmb_copy = [copy(fwd(0), cmb(0), nxt), copy(fwd(1), cmb(1), prv)]

        def send_far(self):
            for c in self.fwd_copy:
                go(c)

        def send_near(self, d):
            go(self.dir_copy[d])

        def relay(self):
            for d in (0, 1):
                self.fwd_copy[d].wait_recv()
                self.add(self.fwd(d), [self.fwd(d), self.block((1, 3)[d], d)])
                go(self.cmb_copy[d])

        def wait(self):
            for c in self.cmb_copy + self.dir_copy:
                c.wait_recv()

        def terms(self, h):
            return [self.block(0, h), self.cmb(h), self.direct(1 - h)]

    def add_bf16(dst, srcs):
        rows = 32

        def step(i, carry):
            r = pl.ds(pl.multiple_of(i * rows, rows), rows)
            total = srcs[0][r, :].astype(jnp.float32)
            for s in srcs[1:]:
                total += s[r, :].astype(jnp.float32)
            dst[r, :] = total.astype(dst.dtype)
            return carry

        lax.fori_loop(0, dst.shape[0] // rows, step, 0)

    def add_f32(dst, srcs):
        rows = 16

        def step(i, carry):
            r = pl.ds(pl.multiple_of(i * rows, rows), rows)
            total = srcs[0][r, :]
            for s in srcs[1:]:
                total += s[r, :]
            dst[r, :] = total
            return carry

        lax.fori_loop(0, dst.shape[0] // rows, step, 0)

    x_far = x_peers[1]
    ring_a = Ring(
        z_next,
        z_prev,
        lambda k, h: part_a.at[(z + k) % 4, pl.ds(h * HALF, HALF)],
        lambda d: fwd_a.at[d],
        lambda d: cmb_a.at[d],
        lambda d: dir_a.at[d],
        add_bf16,
    )
    ring_b = Ring(
        z_next,
        z_prev,
        lambda k, h: part_b.at[xh, (z + k) % 4, pl.ds(h * HALF, HALF)],
        lambda d: fwd_b.at[d],
        lambda d: cmb_b.at[d],
        lambda d: dir_b.at[d],
        add_bf16,
    )
    ax_copy = copy(send_ax, recv_ax, x_far)
    bx_copy = {
        k: copy(part_b.at[1 - xh, (z + k) % 4], recv_bx.at[(z + k) % 4], x_far)
        for k in (2, 1, 3, 0)
    }

    def expert_part(k):
        c = (z + k) % 4
        cols = pl.ds(pl.multiple_of(c * 512, 512), 512)
        loaded(("grd", k))
        for e in (1, 0):
            prod = jnp.dot(
                hmask[e], grd[:, cols], preferred_element_type=jnp.float32
            ).astype(jnp.bfloat16)
            if e == 0:
                part_a[c] = prod
            else:
                part_b[0, c] = prod[:, :256]
                part_b[1, c] = prod[:, 256:]
                go(bx_copy[k])

    d0_copy = {}
    ring_y, ring_z, dx_copy = [], [], []
    for n in range(NCOL):
        for k in range(4):
            c = (y + k) % 4
            d0_copy[k, n] = copy(
                part_d.at[c, :, 1 - core, :, cols_of(n)], acc_d.at[c, :, :, cols_of(n)], sibling
            )
        ring_y.append(
            Ring(
                y_next,
                y_prev,
                lambda k, h, n=n: acc_d.at[(y + k) % 4, h, :, cols_of(n)],
                lambda d, n=n: fwd_y.at[d, :, cols_of(n)],
                lambda d, n=n: cmb_y.at[d, :, cols_of(n)],
                lambda d, n=n: dir_y.at[d, :, cols_of(n)],
                add_f32,
            )
        )
        if n in DIRECT:
            ring_z.append(
                [
                    copy(
                        acc_d.at[
                            y, :, pl.ds(pl.multiple_of((z + k) % 4 * 16, 16), 16), cols_of(n)
                        ],
                        (fwd_z, cmb_z, dir_z)[k - 1].at[:, :, cols_of(n)],
                        dev(x, y, (z + k) % 4, core),
                    )
                    for k in (1, 2, 3)
                ]
            )
        else:
            ring_z.append(
                Ring(
                    z_next,
                    z_prev,
                    lambda k, h, n=n: acc_d.at[
                        y, h, pl.ds(pl.multiple_of((z + k) % 4 * 16, 16), 16), cols_of(n)
                    ],
                    lambda d, n=n: fwd_z.at[d, :, cols_of(n)],
                    lambda d, n=n: cmb_z.at[d, :, cols_of(n)],
                    lambda d, n=n: dir_z.at[d, :, cols_of(n)],
                    add_f32,
                )
            )

        def x_block(k, n=n):
            t = (x + k) % 4
            r = pl.multiple_of(z * 16 + t // 2 * 8, 8)
            return acc_d.at[y, t % 2, pl.ds(r, 8), cols_of(n)]

        dx_copy.append(
            [copy(x_block(k), recv_dx.at[k - 1, :, cols_of(n)], dev((x + k) % 4, y, z, core)) for k in (1, 2, 3)]
        )

    def dense_part(k, n):
        c = (y + k) % 4
        loaded(("val", k), ("att", n))
        lhs = val[:, pl.ds(pl.multiple_of(c * 256, 256), 256)]
        prod = lax.dot_general(lhs, att[:, cols_of(n)], TRANS, preferred_element_type=jnp.float32)
        part_d[c, :, :, :, cols_of(n)] = prod.reshape(2, 2, 64, WIDTHS[n])
        go(d0_copy[k, n])

    def dense_core_sum(k, n):
        c = (y + k) % 4
        d0_copy[k, n].wait_recv()
        for h in (0, 1):
            mine = acc_d.at[c, h, :, cols_of(n)]
            add_f32(mine, [mine, part_d.at[c, h, core, :, cols_of(n)]])
        if k == 2:
            ring_y[n].send_far()
        elif k == 1:
            ring_y[n].send_near(0)
        elif k == 3:
            ring_y[n].send_near(1)

    def fold_b(k):
        bx_copy[k].wait_recv()
        c = (z + k) % 4
        mine = part_b.at[xh, c]
        add_bf16(mine, [mine, recv_bx.at[c]])

    own = pl.ds(pl.multiple_of(xh * 256, 256), 256)
    far = pl.ds(pl.multiple_of((1 - xh) * 256, 256), 256)

    def expert_a_done():
        ring_a.wait()
        for h in (0, 1):
            terms = ring_a.terms(h)

            def step_a(i, carry, h=h, terms=terms):
                r = pl.ds(pl.multiple_of(i * 32, 32), 32)
                o = pl.ds(pl.multiple_of(h * HALF + i * 32, 32), 32)
                send = sum(t[r, far].astype(jnp.float32) for t in terms)
                send_ax[o, :] = send.astype(jnp.bfloat16)
                exp_out[0, o, :] = sum(t[r, own].astype(jnp.float32) for t in terms)
                return carry

            lax.fori_loop(0, HALF // 32, step_a, 0)
        go(ax_copy)

    def dense_y_done(n):
        ring_y[n].wait()
        for h in (0, 1):
            terms = ring_y[n].terms(h)
            add_f32(terms[0], terms)
        if n in DIRECT:
            for k in (1, 0, 2):
                go(ring_z[n][k])
            return
        ring_z[n].send_far()
        ring_z[n].send_near(0)
        ring_z[n].send_near(1)

    def dense_z_done(n):
        if n in DIRECT:
            for c in ring_z[n]:
                c.wait_recv()
        else:
            ring_z[n].wait()
        for h in (0, 1):
            if n in DIRECT:
                mine = acc_d.at[y, h, pl.ds(pl.multiple_of(z * 16, 16), 16), cols_of(n)]
                terms = [mine] + [b.at[h, :, cols_of(n)] for b in (fwd_z, cmb_z, dir_z)]
            else:
                terms = ring_z[n].terms(h)
            add_f32(terms[0], terms)
        for c in dx_copy[n]:
            go(c)

    sums = {"wide": jnp.zeros((32, 256), jnp.float32), "tile": jnp.zeros((8, 128), jnp.float32)}

    def expert_b_done():
        ring_b.wait()
        for h in (0, 1):
            terms = ring_b.terms(h)

            def step_b(i, sq, h=h, terms=terms):
                r = pl.ds(pl.multiple_of(i * 32, 32), 32)
                o = pl.ds(pl.multiple_of(h * HALF + i * 32, 32), 32)
                total = sum(t[r, :].astype(jnp.float32) for t in terms)
                exp_out[1, o, :] = total
                return sq + total * total

            sums["wide"] = lax.fori_loop(0, HALF // 32, step_b, sums["wide"])

    def expert_a_last():
        ax_copy.wait_recv()

        def step_c(i, sq):
            r = pl.ds(pl.multiple_of(i * 32, 32), 32)
            total = exp_out[0, r, :] + recv_ax[r, :].astype(jnp.float32)
            exp_out[0, r, :] = total
            return sq + total * total

        sums["wide"] = lax.fori_loop(0, FFW // 32, step_c, sums["wide"])

    def dense_last(n):
        for c in dx_copy[n]:
            c.wait_recv()
        r = pl.multiple_of(z * 16 + xh * 8, 8)
        total = acc_d[y, xl, pl.ds(r, 8), cols_of(n)]
        for k in range(3):
            total = total + recv_dx[k, :, cols_of(n)]
        den_out[:, cols_of(n)] = total
        sq = total * total
        for j in range(WIDTHS[n] // 128):
            sums["tile"] = sums["tile"] + sq[:, j * 128 : (j + 1) * 128]

    dense_part(2, 0)
    expert_part(2)
    expert_part(3)
    ring_a.send_far()
    enter()
    expert_part(1)
    dense_part(2, 1)
    ring_a.send_near(1)
    dense_core_sum(2, 0)
    dense_part(1, 0)
    dense_part(1, 1)
    ring_a.send_near(0)
    dense_core_sum(2, 1)
    dense_part(3, 0)
    dense_part(3, 1)
    dense_core_sum(3, 0)
    dense_part(2, 2)
    dense_part(0, 3)
    dense_core_sum(1, 1)
    dense_part(0, 2)
    dense_core_sum(1, 0)
    ring_y[0].relay()
    ring_a.relay()
    dense_core_sum(3, 1)
    dense_part(3, 2)
    expert_part(0)
    dense_part(0, 0)
    dense_part(2, 3)
    dense_part(1, 2)
    dense_core_sum(2, 2)
    dense_part(0, 1)
    ring_y[1].relay()
    fold_b(2)
    dense_core_sum(0, 3)
    dense_part(3, 3)
    dense_core_sum(0, 1)
    dense_core_sum(0, 0)
    fold_b(3)
    dense_core_sum(3, 2)
    dense_y_done(0)
    dense_core_sum(1, 2)
    dense_core_sum(2, 3)
    dense_part(1, 3)
    ring_b.send_far()
    ring_y[2].relay()
    dense_core_sum(3, 3)
    ring_z[0].relay()
    dense_core_sum(0, 2)
    dense_y_done(1)
    dense_core_sum(1, 3)
    fold_b(1)
    ring_b.relay()
    dense_z_done(0)
    expert_a_done()
    ring_y[3].relay()
    ring_z[1].relay()
    fold_b(0)
    dense_last(0)
    dense_y_done(2)
    dense_y_done(3)
    ring_b.send_near(0)
    ring_b.send_near(1)
    dense_z_done(1)
    dense_z_done(2)
    dense_z_done(3)
    dense_last(1)
    expert_a_last()
    dense_last(2)
    expert_b_done()
    settle()
    dense_last(3)

    tile = sums["wide"][:, :128] + sums["wide"][:, 128:]
    tile = sums["tile"] + tile[0:8] + tile[8:16] + tile[16:24] + tile[24:32]
    tile = jnp.sum(tile, axis=0, keepdims=True)
    sq_own[...] = tile
    n1 = [copy(sq_own, recv_n1.at[k], edp_peers[k]) for k in range(7)]
    for c in n1:
        go(c)
    for k, c in enumerate(n1):
        c.wait_recv()
        tile = tile + recv_n1[k]
    sq_row[...] = tile
    n2 = [copy(sq_row, recv_n2.at[k], ep_peers[k]) for k in range(15)]
    for c in n2:
        go(c)
    settle()
    for k, c in enumerate(n2):
        c.wait_recv()
        tile = tile + recv_n2[k]
    norm = jnp.sqrt(jnp.sum(tile, axis=1, keepdims=True))
    factor = jnp.minimum(1.0, jnp.sqrt(jnp.full((1, 1), total_count, jnp.float32)) / (norm + 1e-06))
    fac_out[...] = jnp.broadcast_to(factor, (8, 128))


def summed_grads(hid_t, grd, counts, offsets, val, att, total_count):
    vm = pltpu.VMEM
    bf = jnp.bfloat16
    f32 = jnp.float32
    hbm = pl.BlockSpec(memory_space=pltpu.HBM)
    smem = pl.BlockSpec(memory_space=pltpu.SMEM)
    vmem = pl.BlockSpec(memory_space=pltpu.VMEM)
    return pl.pallas_call(
        lambda *refs: grad_kernel(total_count, *refs),
        name="summed_grads",
        out_shape=(
            jax.ShapeDtypeStruct((2, FFW, 256), f32),
            jax.ShapeDtypeStruct((8, D), f32),
            jax.ShapeDtypeStruct((8, 128), f32),
        ),
        in_specs=[smem, smem, hbm, hbm, hbm, hbm],
        out_specs=(vmem, vmem, vmem),
        scratch_shapes=[
            vm((FFW, 1024), bf),
            vm((1024, D), bf),
            vm((2048, HW), bf),
            vm((2048, D), bf),
            vm((2, FFW, 1024), bf),
            vm((4, FFW, 512), bf),
            vm((2, 4, FFW, 256), bf),
            vm((4, FFW, 256), bf),
            vm((2, HALF, 512), bf),
            vm((2, HALF, 512), bf),
            vm((2, HALF, 512), bf),
            vm((FFW, 256), bf),
            vm((FFW, 256), bf),
            vm((2, HALF, 256), bf),
            vm((2, HALF, 256), bf),
            vm((2, HALF, 256), bf),
            vm((4, 2, 2, 64, D), f32),
            vm((4, 2, 64, D), f32),
            vm((2, 64, D), f32),
            vm((2, 64, D), f32),
            vm((2, 64, D), f32),
            vm((2, 16, D), f32),
            vm((2, 16, D), f32),
            vm((2, 16, D), f32),
            vm((3, 8, D), f32),
            vm((1, 128), f32),
            vm((1, 128), f32),
            vm((7, 1, 128), f32),
            vm((15, 1, 128), f32),
            pltpu.SemaphoreType.DMA((13,)),
            pltpu.SemaphoreType.DMA((115,)),
            pltpu.SemaphoreType.DMA((115,)),
        ],
        compiler_params=pltpu.CompilerParams(
            collective_id=0, has_side_effects=True, vmem_limit_bytes=52 << 20
        ),
    )(counts, offsets, hid_t, grd, val, att)


STEPS = 11


def adam_kernel(fac, eg, ew, em, es, dg, dw, dm, ds, *rest):
    outs, (ow, om, os_, pw, pm, ps), sem = rest[:6], rest[6:12], rest[12]
    factor = fac[0:1, 0:1]
    copies = []

    def out(src, dst):
        copies.append(pltpu.make_async_copy(src, dst, sem.at[len(copies)]))
        copies[-1].start()

    pw[...], pm[...], ps[...] = adamw(dw[...], dm[...], ds[...], dg[...], factor)
    for src, dst in zip((pw, pm, ps), outs[3:]):
        out(src, dst)
    rows = EXP_DEV * FFW // STEPS
    for i in range(STEPS):
        r = pl.ds(i * rows, rows)
        ow[r], om[r], os_[r] = adamw(ew[r], em[r], es[r], eg[r], factor)
        for src, dst in zip((ow, om, os_), outs[:3]):
            out(src.at[r], dst.at[r])
    for c in copies:
        c.wait()


def updated(factor, expert, dense):
    rows = EXP_DEV * FFW
    vmem = pl.BlockSpec(memory_space=pltpu.VMEM)
    hbm = pl.BlockSpec(memory_space=pl.ANY)
    return pl.pallas_call(
        adam_kernel,
        name="clipped_adamw",
        out_shape=[jax.ShapeDtypeStruct((rows, 256), jnp.float32)] * 3
        + [jax.ShapeDtypeStruct((8, D), jnp.float32)] * 3,
        in_specs=[vmem] * 9,
        out_specs=[hbm] * 6,
        scratch_shapes=[pltpu.VMEM((rows, 256), jnp.float32)] * 3
        + [pltpu.VMEM((8, D), jnp.float32)] * 3
        + [pltpu.SemaphoreType.DMA((3 * STEPS + 3,))],
        compiler_params=pltpu.CompilerParams(vmem_limit_bytes=16 << 20),
    )(factor, *expert, *dense)


def body(
    routed_hidden,
    routed_grads,
    expert_counts,
    expert_offsets,
    attn_values,
    attn_grads,
    expert_master,
    expert_moment,
    expert_second,
    dense_master,
    dense_moment,
    dense_second,
):
    total_count = float(LAYERS * EXP_DEV * lax.axis_size("ep") * FFW * D + LAYERS * HW * D)
    expert_total, dense_total, factor = summed_grads(
        routed_hidden[0, 0].T,
        routed_grads[0, 0],
        expert_counts[0, 0],
        expert_offsets[0, 0],
        attn_values[0],
        attn_grads[0],
        total_count,
    )
    expert = [
        a.reshape(EXP_DEV * FFW, 256)
        for a in (expert_total, expert_master, expert_moment, expert_second)
    ]
    dense = [a.reshape(8, D) for a in (dense_total, dense_master, dense_moment, dense_second)]
    new = updated(factor, expert, dense)
    return tuple(a.reshape(expert_master.shape) for a in new[:3]) + tuple(
        a.reshape(dense_master.shape) for a in new[3:]
    )


def solution(mesh):
    return jax.shard_map(
        body,
        mesh=mesh,
        in_specs=(
            P(None, "ep", "edp", None),
            P(None, "ep", "edp", None),
            P(None, "edp", "ep"),
            P(None, "edp", "ep"),
            P(None, ("ep", "edp"), None),
            P(None, ("ep", "edp"), None),
            P(None, "ep", None, "edp"),
            P(None, "ep", None, "edp"),
            P(None, "ep", None, "edp"),
            P(None, ("ep", "edp"), None),
            P(None, ("ep", "edp"), None),
            P(None, ("ep", "edp"), None),
        ),
        out_specs=(
            P(None, "ep", None, "edp"),
            P(None, "ep", None, "edp"),
            P(None, "ep", None, "edp"),
            P(None, ("ep", "edp"), None),
            P(None, ("ep", "edp"), None),
            P(None, ("ep", "edp"), None),
        ),
        check_vma=False,
    )
```

```python
import jax
import jax.numpy as jnp
from jax import lax
from jax.experimental import pallas as pl
from jax.experimental.pallas import tpu as pltpu
from jax.sharding import PartitionSpec as P

D = 2048
FFW = 704
HW = 1024
LAYERS = 1
EXP_DEV = 2
HALF = FFW // 2
WIDTHS = (512, 768, 512, 256)
NCOL = len(WIDTHS)
DIRECT = (2, 3)

beta_one = 0.9
beta_two = 0.95
adam_step = 10.0
adam_eps = 1e-08
learn_rate = 0.01
decay_rate = 0.1

MESH = pl.DeviceIdType.MESH
TRANS = (((0,), (0,)), ((), ()))


def adamw(master, moment, second, grad, factor):
    clipped = grad * factor
    new_moment = beta_one * moment + (1.0 - beta_one) * clipped
    new_second = beta_two * second + (1.0 - beta_two) * clipped * clipped
    corr_one = 1.0 - beta_one**adam_step
    corr_two = 1.0 - beta_two**adam_step
    update = (
        new_moment / corr_one / (jnp.sqrt(new_second / corr_two) + adam_eps) + decay_rate * master
    )
    return (master - learn_rate * update, new_moment, new_second)


def grad_kernel(
    total_count,
    segments,
    hid_hbm,
    grd_hbm,
    val_hbm,
    att_hbm,
    exp_out,
    den_out,
    fac_out,
    hid,
    grd,
    val,
    att,
    hmask,
    part_a,
    part_b,
    recv_bx,
    fwd_a,
    cmb_a,
    dir_a,
    send_ax,
    recv_ax,
    fwd_b,
    cmb_b,
    dir_b,
    part_d,
    acc_d,
    fwd_y,
    cmb_y,
    dir_y,
    fwd_z,
    cmb_z,
    dir_z,
    recv_dx,
    sq_own,
    sq_row,
    recv_n1,
    recv_n2,
    load_sem,
    send_sem,
    recv_sem,
):
    ep = lax.axis_index("ep")
    edp = lax.axis_index("edp")
    y = ep // 4
    xl = (ep // 2) % 2
    core = ep % 2
    z = edp // 2
    xh = edp % 2
    x = xh * 2 + xl

    def dev(px, py, pz, pc):
        return (py * 4 + (px % 2) * 2 + pc, pz * 2 + px // 2)

    sibling = dev(x, y, z, 1 - core)
    z_next = dev(x, y, (z + 1) % 4, core)
    z_prev = dev(x, y, (z + 3) % 4, core)
    y_next = dev(x, (y + 1) % 4, z, core)
    y_prev = dev(x, (y + 3) % 4, z, core)

    barrier = pltpu.get_barrier_semaphore()
    ep_peers = [((ep + k) % 16, edp) for k in range(1, 16)]
    edp_peers = [(ep, (edp + k) % 8) for k in range(1, 8)]
    x_peers = [dev((x + k) % 4, y, z, core) for k in (1, 2, 3)]
    greeted = [sibling, y_next, y_prev, z_next, z_prev] + x_peers
    for peer in greeted:
        pl.semaphore_signal(barrier, inc=1, device_id=peer, device_id_type=MESH)

    def cols_of(n):
        return pl.ds(sum(WIDTHS[:n]), WIDTHS[n])

    loads = {}

    def load(key, src, dst):
        loads[key] = pltpu.make_async_copy(src, dst, load_sem.at[len(loads)])
        loads[key].start()

    def load_columns(key, src, dst, start, width):
        cols = pl.ds(pl.multiple_of(start, width), width)
        load(key, src.at[:, cols], dst.at[:, cols])

    load("hid", hid_hbm, hid)
    load_columns(("grd", 2), grd_hbm, grd, (z + 2) % 4 * 512, 512)
    load_columns(("val", 2), val_hbm, val, (y + 2) % 4 * 256, 256)
    load(("att", 0), att_hbm.at[:, cols_of(0)], att.at[:, cols_of(0)])
    for k in (1, 3, 0):
        load_columns(("val", k), val_hbm, val, (y + k) % 4 * 256, 256)
        load_columns(("grd", k), grd_hbm, grd, (z + k) % 4 * 512, 512)
        if k != 0:
            n = (k + 1) // 2
            load(("att", n), att_hbm.at[:, cols_of(n)], att.at[:, cols_of(n)])
    load(("att", 3), att_hbm.at[:, cols_of(3)], att.at[:, cols_of(3)])
    used = set()

    def loaded(*keys):
        for key in keys:
            if key not in used:
                used.add(key)
                loads[key].wait()

    loaded("hid")
    lane = lax.broadcasted_iota(jnp.int32, (FFW, 1024), 1)
    for e in range(EXP_DEV):
        rel = lane - segments[EXP_DEV + e]
        keep = jnp.logical_and(rel >= 0, rel < segments[e])
        hmask[e] = jnp.where(keep, hid[...], jnp.zeros_like(hid))

    started = []
    free = iter(range(200))

    def copy(src, dst, peer):
        i = next(free)
        return pltpu.make_async_remote_copy(
            src_ref=src,
            dst_ref=dst,
            send_sem=send_sem.at[i],
            recv_sem=recv_sem.at[i],
            device_id=peer,
            device_id_type=MESH,
        )

    held = []

    def go(c):
        if held is not None:
            held.append(c)
        else:
            c.start()
        started.append(c)

    def enter():
        nonlocal held
        pl.semaphore_wait(barrier, len(greeted))
        for c in held:
            c.start()
        held = None

    def settle():
        while started:
            started.pop(0).wait_send()

    class Ring:
        def __init__(self, nxt, prv, block, fwd, cmb, direct, add):
            self.block, self.fwd, self.cmb, self.direct, self.add = block, fwd, cmb, direct, add
            self.fwd_copy = [copy(block(2, 0), fwd(0), nxt), copy(block(2, 1), fwd(1), prv)]
            self.dir_copy = [copy(block(1, 1), direct(0), nxt), copy(block(3, 0), direct(1), prv)]
            self.cmb_copy = [copy(fwd(0), cmb(0), nxt), copy(fwd(1), cmb(1), prv)]

        def send_far(self):
            for c in self.fwd_copy:
                go(c)

        def send_near(self, d):
            go(self.dir_copy[d])

        def relay(self):
            for d in (0, 1):
                self.fwd_copy[d].wait_recv()
                self.add(self.fwd(d), [self.fwd(d), self.block((1, 3)[d], d)])
                go(self.cmb_copy[d])

        def wait(self):
            for c in self.cmb_copy + self.dir_copy:
                c.wait_recv()

        def terms(self, h):
            return [self.block(0, h), self.cmb(h), self.direct(1 - h)]

    def add_bf16(dst, srcs):
        rows = 32

        def step(i, carry):
            r = pl.ds(pl.multiple_of(i * rows, rows), rows)
            total = srcs[0][r, :].astype(jnp.float32)
            for s in srcs[1:]:
                total += s[r, :].astype(jnp.float32)
            dst[r, :] = total.astype(dst.dtype)
            return carry

        lax.fori_loop(0, dst.shape[0] // rows, step, 0)

    def add_f32(dst, srcs):
        rows = 16

        def step(i, carry):
            r = pl.ds(pl.multiple_of(i * rows, rows), rows)
            total = srcs[0][r, :]
            for s in srcs[1:]:
                total += s[r, :]
            dst[r, :] = total
            return carry

        lax.fori_loop(0, dst.shape[0] // rows, step, 0)

    x_far = x_peers[1]
    ring_a = Ring(
        z_next,
        z_prev,
        lambda k, h: part_a.at[(z + k) % 4, pl.ds(h * HALF, HALF)],
        lambda d: fwd_a.at[d],
        lambda d: cmb_a.at[d],
        lambda d: dir_a.at[d],
        add_bf16,
    )
    ring_b = Ring(
        z_next,
        z_prev,
        lambda k, h: part_b.at[xh, (z + k) % 4, pl.ds(h * HALF, HALF)],
        lambda d: fwd_b.at[d],
        lambda d: cmb_b.at[d],
        lambda d: dir_b.at[d],
        add_bf16,
    )
    ax_copy = copy(send_ax, recv_ax, x_far)
    bx_copy = {
        k: copy(part_b.at[1 - xh, (z + k) % 4], recv_bx.at[(z + k) % 4], x_far)
        for k in (2, 1, 3, 0)
    }

    def expert_part(k):
        c = (z + k) % 4
        cols = pl.ds(pl.multiple_of(c * 512, 512), 512)
        loaded(("grd", k))
        for e in (1, 0):
            prod = jnp.dot(
                hmask[e], grd[:, cols], preferred_element_type=jnp.float32
            ).astype(jnp.bfloat16)
            if e == 0:
                part_a[c] = prod
            else:
                part_b[0, c] = prod[:, :256]
                part_b[1, c] = prod[:, 256:]
                go(bx_copy[k])

    d0_copy = {}
    ring_y, ring_z, dx_copy = [], [], []
    for n in range(NCOL):
        for k in range(4):
            c = (y + k) % 4
            d0_copy[k, n] = copy(
                part_d.at[c, :, 1 - core, :, cols_of(n)], acc_d.at[c, :, :, cols_of(n)], sibling
            )
        ring_y.append(
            Ring(
                y_next,
                y_prev,
                lambda k, h, n=n: acc_d.at[(y + k) % 4, h, :, cols_of(n)],
                lambda d, n=n: fwd_y.at[d, :, cols_of(n)],
                lambda d, n=n: cmb_y.at[d, :, cols_of(n)],
                lambda d, n=n: dir_y.at[d, :, cols_of(n)],
                add_f32,
            )
        )
        if n in DIRECT:
            ring_z.append(
                [
                    copy(
                        acc_d.at[
                            y, :, pl.ds(pl.multiple_of((z + k) % 4 * 16, 16), 16), cols_of(n)
                        ],
                        (fwd_z, cmb_z, dir_z)[k - 1].at[:, :, cols_of(n)],
                        dev(x, y, (z + k) % 4, core),
                    )
                    for k in (1, 2, 3)
                ]
            )
        else:
            ring_z.append(
                Ring(
                    z_next,
                    z_prev,
                    lambda k, h, n=n: acc_d.at[
                        y, h, pl.ds(pl.multiple_of((z + k) % 4 * 16, 16), 16), cols_of(n)
                    ],
                    lambda d, n=n: fwd_z.at[d, :, cols_of(n)],
                    lambda d, n=n: cmb_z.at[d, :, cols_of(n)],
                    lambda d, n=n: dir_z.at[d, :, cols_of(n)],
                    add_f32,
                )
            )

        def x_block(k, n=n):
            t = (x + k) % 4
            r = pl.multiple_of(z * 16 + t // 2 * 8, 8)
            return acc_d.at[y, t % 2, pl.ds(r, 8), cols_of(n)]

        dx_copy.append(
            [copy(x_block(k), recv_dx.at[k - 1, :, cols_of(n)], dev((x + k) % 4, y, z, core)) for k in (1, 2, 3)]
        )

    def dense_part(k, n):
        c = (y + k) % 4
        loaded(("val", k), ("att", n))
        lhs = val[:, pl.ds(pl.multiple_of(c * 256, 256), 256)]
        prod = lax.dot_general(lhs, att[:, cols_of(n)], TRANS, preferred_element_type=jnp.float32)
        part_d[c, :, :, :, cols_of(n)] = prod.reshape(2, 2, 64, WIDTHS[n])
        go(d0_copy[k, n])

    def dense_core_sum(k, n):
        c = (y + k) % 4
        d0_copy[k, n].wait_recv()
        for h in (0, 1):
            mine = acc_d.at[c, h, :, cols_of(n)]
            add_f32(mine, [mine, part_d.at[c, h, core, :, cols_of(n)]])
        if k == 2:
            ring_y[n].send_far()
        elif k == 1:
            ring_y[n].send_near(0)
        elif k == 3:
            ring_y[n].send_near(1)

    def fold_b(k):
        bx_copy[k].wait_recv()
        c = (z + k) % 4
        mine = part_b.at[xh, c]
        add_bf16(mine, [mine, recv_bx.at[c]])

    own = pl.ds(pl.multiple_of(xh * 256, 256), 256)
    far = pl.ds(pl.multiple_of((1 - xh) * 256, 256), 256)

    def expert_a_done():
        ring_a.wait()
        for h in (0, 1):
            terms = ring_a.terms(h)

            def step_a(i, carry, h=h, terms=terms):
                r = pl.ds(pl.multiple_of(i * 32, 32), 32)
                o = pl.ds(pl.multiple_of(h * HALF + i * 32, 32), 32)
                send = sum(t[r, far].astype(jnp.float32) for t in terms)
                send_ax[o, :] = send.astype(jnp.bfloat16)
                exp_out[0, o, :] = sum(t[r, own].astype(jnp.float32) for t in terms)
                return carry

            lax.fori_loop(0, HALF // 32, step_a, 0)
        go(ax_copy)

    def dense_y_done(n):
        ring_y[n].wait()
        for h in (0, 1):
            terms = ring_y[n].terms(h)
            add_f32(terms[0], terms)
        if n in DIRECT:
            for k in (1, 0, 2):
                go(ring_z[n][k])
            return
        ring_z[n].send_far()
        ring_z[n].send_near(0)
        ring_z[n].send_near(1)

    def dense_z_done(n):
        if n in DIRECT:
            for c in ring_z[n]:
                c.wait_recv()
        else:
            ring_z[n].wait()
        for h in (0, 1):
            if n in DIRECT:
                mine = acc_d.at[y, h, pl.ds(pl.multiple_of(z * 16, 16), 16), cols_of(n)]
                terms = [mine] + [b.at[h, :, cols_of(n)] for b in (fwd_z, cmb_z, dir_z)]
            else:
                terms = ring_z[n].terms(h)
            add_f32(terms[0], terms)
        for c in dx_copy[n]:
            go(c)

    sums = {"wide": jnp.zeros((32, 256), jnp.float32), "tile": jnp.zeros((8, 128), jnp.float32)}

    def expert_b_done():
        ring_b.wait()
        for h in (0, 1):
            terms = ring_b.terms(h)

            def step_b(i, sq, h=h, terms=terms):
                r = pl.ds(pl.multiple_of(i * 32, 32), 32)
                o = pl.ds(pl.multiple_of(h * HALF + i * 32, 32), 32)
                total = sum(t[r, :].astype(jnp.float32) for t in terms)
                exp_out[1, o, :] = total
                return sq + total * total

            sums["wide"] = lax.fori_loop(0, HALF // 32, step_b, sums["wide"])

    def expert_a_last():
        ax_copy.wait_recv()

        def step_c(i, sq):
            r = pl.ds(pl.multiple_of(i * 32, 32), 32)
            total = exp_out[0, r, :] + recv_ax[r, :].astype(jnp.float32)
            exp_out[0, r, :] = total
            return sq + total * total

        sums["wide"] = lax.fori_loop(0, FFW // 32, step_c, sums["wide"])

    def dense_last(n):
        for c in dx_copy[n]:
            c.wait_recv()
        r = pl.multiple_of(z * 16 + xh * 8, 8)
        total = acc_d[y, xl, pl.ds(r, 8), cols_of(n)]
        for k in range(3):
            total = total + recv_dx[k, :, cols_of(n)]
        den_out[:, cols_of(n)] = total
        sq = total * total
        for j in range(WIDTHS[n] // 128):
            sums["tile"] = sums["tile"] + sq[:, j * 128 : (j + 1) * 128]

    dense_part(2, 0)
    expert_part(2)
    expert_part(3)
    ring_a.send_far()
    enter()
    expert_part(1)
    dense_part(2, 1)
    ring_a.send_near(1)
    dense_core_sum(2, 0)
    dense_part(1, 0)
    dense_part(1, 1)
    ring_a.send_near(0)
    dense_core_sum(2, 1)
    dense_part(3, 0)
    dense_part(3, 1)
    dense_core_sum(3, 0)
    dense_part(2, 2)
    dense_part(0, 3)
    dense_core_sum(1, 1)
    dense_part(0, 2)
    dense_core_sum(1, 0)
    ring_y[0].relay()
    ring_a.relay()
    dense_core_sum(3, 1)
    dense_part(3, 2)
    expert_part(0)
    dense_part(0, 0)
    dense_part(2, 3)
    dense_part(1, 2)
    dense_core_sum(2, 2)
    dense_part(0, 1)
    ring_y[1].relay()
    fold_b(2)
    dense_core_sum(0, 3)
    dense_part(3, 3)
    dense_core_sum(0, 1)
    dense_core_sum(0, 0)
    fold_b(3)
    dense_core_sum(3, 2)
    dense_y_done(0)
    dense_core_sum(1, 2)
    dense_core_sum(2, 3)
    dense_part(1, 3)
    ring_b.send_far()
    ring_y[2].relay()
    dense_core_sum(3, 3)
    ring_z[0].relay()
    dense_core_sum(0, 2)
    dense_y_done(1)
    dense_core_sum(1, 3)
    fold_b(1)
    ring_b.relay()
    dense_z_done(0)
    expert_a_done()
    ring_y[3].relay()
    ring_z[1].relay()
    fold_b(0)
    dense_last(0)
    dense_y_done(2)
    dense_y_done(3)
    ring_b.send_near(0)
    ring_b.send_near(1)
    dense_z_done(1)
    dense_z_done(2)
    dense_z_done(3)
    dense_last(1)
    expert_a_last()
    dense_last(2)
    expert_b_done()
    settle()
    dense_last(3)

    tile = sums["wide"][:, :128] + sums["wide"][:, 128:]
    tile = sums["tile"] + tile[0:8] + tile[8:16] + tile[16:24] + tile[24:32]
    tile = jnp.sum(tile, axis=0, keepdims=True)
    sq_own[...] = tile
    n1 = [copy(sq_own, recv_n1.at[k], edp_peers[k]) for k in range(7)]
    for c in n1:
        go(c)
    for k, c in enumerate(n1):
        c.wait_recv()
        tile = tile + recv_n1[k]
    sq_row[...] = tile
    n2 = [copy(sq_row, recv_n2.at[k], ep_peers[k]) for k in range(15)]
    for c in n2:
        go(c)
    settle()
    for k, c in enumerate(n2):
        c.wait_recv()
        tile = tile + recv_n2[k]
    norm = jnp.sqrt(jnp.sum(tile, axis=1, keepdims=True))
    factor = jnp.minimum(1.0, jnp.sqrt(jnp.full((1, 1), total_count, jnp.float32)) / (norm + 1e-06))
    fac_out[...] = jnp.broadcast_to(factor, (8, 128))


def summed_grads(hid_t, grd, segments, val, att, total_count):
    vm = pltpu.VMEM
    bf = jnp.bfloat16
    f32 = jnp.float32
    hbm = pl.BlockSpec(memory_space=pltpu.HBM)
    smem = pl.BlockSpec(memory_space=pltpu.SMEM)
    vmem = pl.BlockSpec(memory_space=pltpu.VMEM)
    return pl.pallas_call(
        lambda *refs: grad_kernel(total_count, *refs),
        name="summed_grads",
        out_shape=(
            jax.ShapeDtypeStruct((2, FFW, 256), f32),
            jax.ShapeDtypeStruct((8, D), f32),
            jax.ShapeDtypeStruct((8, 128), f32),
        ),
        in_specs=[smem, hbm, hbm, hbm, hbm],
        out_specs=(vmem, vmem, vmem),
        scratch_shapes=[
            vm((FFW, 1024), bf),
            vm((1024, D), bf),
            vm((2048, HW), bf),
            vm((2048, D), bf),
            vm((2, FFW, 1024), bf),
            vm((4, FFW, 512), bf),
            vm((2, 4, FFW, 256), bf),
            vm((4, FFW, 256), bf),
            vm((2, HALF, 512), bf),
            vm((2, HALF, 512), bf),
            vm((2, HALF, 512), bf),
            vm((FFW, 256), bf),
            vm((FFW, 256), bf),
            vm((2, HALF, 256), bf),
            vm((2, HALF, 256), bf),
            vm((2, HALF, 256), bf),
            vm((4, 2, 2, 64, D), f32),
            vm((4, 2, 64, D), f32),
            vm((2, 64, D), f32),
            vm((2, 64, D), f32),
            vm((2, 64, D), f32),
            vm((2, 16, D), f32),
            vm((2, 16, D), f32),
            vm((2, 16, D), f32),
            vm((3, 8, D), f32),
            vm((1, 128), f32),
            vm((1, 128), f32),
            vm((7, 1, 128), f32),
            vm((15, 1, 128), f32),
            pltpu.SemaphoreType.DMA((13,)),
            pltpu.SemaphoreType.DMA((115,)),
            pltpu.SemaphoreType.DMA((115,)),
        ],
        compiler_params=pltpu.CompilerParams(
            collective_id=0, has_side_effects=True, vmem_limit_bytes=52 << 20
        ),
    )(segments, hid_t, grd, val, att)


STEPS = 11


def adam_kernel(fac, eg, ew, em, es, dg, dw, dm, ds, *rest):
    outs, (ow, om, os_, pw, pm, ps), sem = rest[:6], rest[6:12], rest[12]
    factor = fac[0:1, 0:1]
    copies = []

    def out(src, dst):
        copies.append(pltpu.make_async_copy(src, dst, sem.at[len(copies)]))
        copies[-1].start()

    pw[...], pm[...], ps[...] = adamw(dw[...], dm[...], ds[...], dg[...], factor)
    for src, dst in zip((pw, pm, ps), outs[3:]):
        out(src, dst)
    rows = EXP_DEV * FFW // STEPS
    for i in range(STEPS):
        r = pl.ds(i * rows, rows)
        ow[r], om[r], os_[r] = adamw(ew[r], em[r], es[r], eg[r], factor)
        for src, dst in zip((ow, om, os_), outs[:3]):
            out(src.at[r], dst.at[r])
    for c in copies:
        c.wait()


def updated(factor, expert, dense):
    rows = EXP_DEV * FFW
    vmem = pl.BlockSpec(memory_space=pltpu.VMEM)
    hbm = pl.BlockSpec(memory_space=pl.ANY)
    return pl.pallas_call(
        adam_kernel,
        name="clipped_adamw",
        out_shape=[jax.ShapeDtypeStruct((rows, 256), jnp.float32)] * 3
        + [jax.ShapeDtypeStruct((8, D), jnp.float32)] * 3,
        in_specs=[vmem] * 9,
        out_specs=[hbm] * 6,
        scratch_shapes=[pltpu.VMEM((rows, 256), jnp.float32)] * 3
        + [pltpu.VMEM((8, D), jnp.float32)] * 3
        + [pltpu.SemaphoreType.DMA((3 * STEPS + 3,))],
        compiler_params=pltpu.CompilerParams(vmem_limit_bytes=16 << 20),
    )(factor, *expert, *dense)


def body(
    routed_hidden,
    routed_grads,
    expert_counts,
    expert_offsets,
    attn_values,
    attn_grads,
    expert_master,
    expert_moment,
    expert_second,
    dense_master,
    dense_moment,
    dense_second,
):
    total_count = float(LAYERS * EXP_DEV * lax.axis_size("ep") * FFW * D + LAYERS * HW * D)
    expert_total, dense_total, factor = summed_grads(
        routed_hidden[0, 0].T,
        routed_grads[0, 0],
        jnp.concatenate([expert_counts[0, 0], expert_offsets[0, 0]]),
        attn_values[0],
        attn_grads[0],
        total_count,
    )
    expert = [
        a.reshape(EXP_DEV * FFW, 256)
        for a in (expert_total, expert_master, expert_moment, expert_second)
    ]
    dense = [a.reshape(8, D) for a in (dense_total, dense_master, dense_moment, dense_second)]
    new = updated(factor, expert, dense)
    return tuple(a.reshape(expert_master.shape) for a in new[:3]) + tuple(
        a.reshape(dense_master.shape) for a in new[3:]
    )


def solution(mesh):
    return jax.shard_map(
        body,
        mesh=mesh,
        in_specs=(
            P(None, "ep", "edp", None),
            P(None, "ep", "edp", None),
            P(None, "edp", "ep"),
            P(None, "edp", "ep"),
            P(None, ("ep", "edp"), None),
            P(None, ("ep", "edp"), None),
            P(None, "ep", None, "edp"),
            P(None, "ep", None, "edp"),
            P(None, "ep", None, "edp"),
            P(None, ("ep", "edp"), None),
            P(None, ("ep", "edp"), None),
            P(None, ("ep", "edp"), None),
        ),
        out_specs=(
            P(None, "ep", None, "edp"),
            P(None, "ep", None, "edp"),
            P(None, "ep", None, "edp"),
            P(None, ("ep", "edp"), None),
            P(None, ("ep", "edp"), None),
            P(None, ("ep", "edp"), None),
        ),
        check_vma=False,
    )
```
